128 devices in a mesh: expert: 16 (over z, y), tensor: 8 (over x, core).
Axes of the slice: x: 4, y: 4, z: 4, core: 2. Of those that a mesh axis runs over, the one named last changes fastest.
Arguments:
- tokens: bfloat16 [2048, 8192], P('expert', 'tensor'), may hold values from -25 to 25, as said below
- routes: int32 [2048, 2], P('expert'), may hold values from 0 to 15, all different within a row; in each aligned block of 128 rows (0 to 127, 128 to 255, ...) at most 24 rows name the same one
- norm_gain: float32 [2, 8192], P(None, 'tensor'), may hold values from 0.5 to 1.5
- router_weight: bfloat16 [2, 8192, 16], P(None, 'tensor'), may hold values from -0.0625 to 0.0625
- gate_codes: int32 [2, 16, 4096, 1024], P(None, 'expert', None, 'tensor'), may hold values from 0 to 255
- gate_scales: int32 [2, 16, 64, 1024], P(None, 'expert', None, 'tensor'), may hold values from 8 to 10
- up_codes: int32 [2, 16, 4096, 1024], P(None, 'expert', None, 'tensor'), may hold values from 0 to 255
- up_scales: int32 [2, 16, 64, 1024], P(None, 'expert', None, 'tensor'), may hold values from 8 to 10
- down_codes: int32 [2, 16, 512, 8192], P(None, 'expert', 'tensor'), may hold values from 0 to 255
- down_scales: int32 [2, 16, 8, 8192], P(None, 'expert', 'tensor'), may hold values from 6 to 8
Outputs:
- hidden_out: bfloat16 [2048, 8192], P('expert', 'tensor')
The draws below stay inside these ranges and needn't reach their ends.
Inputs may be any that keep to these rules, and one draw needn't show every extreme that they name: `routes`: in the rows of one index of expert (128 aligned rows) no expert is named by more than 24 rows, a bound that some block reaches; the two experts of a row differ. `tokens`: token activations.
All inputs are finite; a program needn't handle non-finite values.
Results may differ from the reference program's by a relative error of at most 0.029.
Values may be sent and summed in bfloat16 or wider, within the bound.
A program may use at most 192 MiB of HBM per device.

```python
import math
import jax
import jax.numpy as jnp
import numpy as np
from jax import lax

D = 8192
FF = 1024
GROUP = 128
IN_SHIFT = 9
OUT_SHIFT = 7
LAYERS = 2
TOK_DEV = 128
TOKENS = 2048
EXPERTS = 16
CAP = 24
N_TENSOR = 8


def draw_tokens(key, part):
    columns = jnp.arange(D, dtype=jnp.float32)
    column_ramp = jnp.exp(0.6 * (2.0 * columns / (D - 1) - 1.0))
    values = jnp.clip(jax.random.normal(key, (TOKENS, D), jnp.float32), -6.0, 6.0)
    return (values * column_ramp[None, :]).astype(jnp.bfloat16)


def plant(result, rng, low, top_value):
    shape = result.shape
    index_at = [jax.random.randint(jax.random.fold_in(rng, axis), (), 0, shape[axis]) for axis in range(len(shape))]
    result = result.at[tuple(index_at)].set(low)
    longest = shape.index(max(shape))
    index_at[longest] = (index_at[longest] + 1) % shape[longest]
    return result.at[tuple(index_at)].set(top_value)


def levels(rng, dims, shards, smallest, top_value):
    loudness, own = 1.0, jax.random.fold_in(rng, 6)
    for position, parts in shards:
        steps = jnp.exp(jax.random.uniform(jax.random.fold_in(own, position), (parts,), jnp.float32, smallest / len(shards), top_value / len(shards)))
        loudness = loudness * jnp.repeat(steps, dims[position] // parts).reshape([-1 if axis == position else 1 for axis in range(len(dims))])
    return loudness


def shared_out(rng, own, number, rows, number_of, top, bound, skew):
    ranking = jax.random.permutation(rng, number_of)
    heavy_load, usual = shares(number_of, rows * top, bound, skew, True), shares(number_of, rows * top, bound, skew, False)
    places = jnp.arange(number_of)

    def named(sizes, rotation):
        used = int((sizes > 0).sum())
        fixed = max(1, used // 4)
        shifted = fixed + (places - fixed + rotation * (used - fixed)) % max(1, number_of - fixed)
        return jnp.zeros((number_of,), jnp.int32).at[ranking[jnp.where(places < fixed, places, shifted)]].set(jnp.asarray(sizes, jnp.int32))

    sizes = jnp.where(number % 4 == 0, named(heavy_load, number // 4), named(usual, number - number // 4 - 1))
    mixed = jax.random.permutation(jax.random.fold_in(own, 3), number_of)
    source_of, taker = mixed[0:number_of // 2 * 2:2], mixed[1:number_of // 2 * 2:2]
    margin = jnp.minimum(sizes[source_of] - 1, bound - sizes[taker]) // 2
    margin = jnp.where((source_of == ranking[0]) | (taker == ranking[0]) | (sizes[taker] == 0), 0, jnp.maximum(margin, 0))
    shifted = jax.random.randint(jax.random.fold_in(own, 4), (number_of // 2,), 0, 1 << 20) % (margin + 1)
    sizes = sizes.at[source_of].add(-shifted).at[taker].add(shifted)
    members = jnp.searchsorted(jnp.cumsum(sizes), jnp.arange(rows * top), side="right").astype(jnp.int32)
    grid = members.reshape(top, rows).T
    grid = grid[jax.random.permutation(jax.random.fold_in(own, 1), rows)]
    rotation = jax.random.randint(jax.random.fold_in(own, 2), (rows, 1), 0, top)
    return jnp.take_along_axis(grid, (jnp.arange(top)[None, :] + rotation) % top, axis=1)


def shares(amount, total, limit, slope, full):
    weights = [(1 << 20) // math.isqrt(grade ** slope) + 1 for grade in range(1, amount + 1)]
    largest = limit if full else min(limit, max(-(-total // amount), total * weights[0] // sum(weights)))
    least = 1 if total - largest >= amount - 1 else 0
    holding, surplus = [largest] + [least] * (amount - 1), total - largest - least * (amount - 1)
    while surplus > 0:
        free = [i for i in range(1, amount) if holding[i] < largest] or [i for i in range(1, amount) if holding[i] < limit]
        mass, budget = sum([weights[i] for i in free]), surplus
        for i in free:
            addition = min(limit - holding[i], max(1, budget * weights[i] // mass), surplus)
            holding[i] = holding[i] + addition
            surplus = surplus - addition
    return np.array(holding)


def normal_values(own_key, dims, deviation, bound, pieces=(), kind=jnp.bfloat16):
    values = jax.random.normal(own_key, dims, jnp.float32) * deviation
    if len(pieces) > 0:
        values = levels(own_key, dims, pieces, -0.22, 0.18) * values
    return jnp.clip(values, min=-bound, max=bound).astype(kind)


def setup_inputs(seed: int = 0) -> dict:
    key_of = jax.random.split(jax.random.key(seed), 11)
    tokens = draw_tokens(jax.random.fold_in(key_of[10], 71), 0)
    routes_keys = jax.random.split(jax.random.fold_in(key_of[1], 1), TOKENS // TOK_DEV)
    routes_turns = jax.random.permutation(jax.random.fold_in(key_of[1], 3), TOKENS // TOK_DEV)
    routes = jax.vmap(lambda own, number: shared_out(jax.random.fold_in(key_of[1], 2), own, number, TOK_DEV, EXPERTS, 2, CAP, 2))(routes_keys, routes_turns).reshape((TOKENS, 2))
    norm_gain = jnp.clip(1.0 + 0.1 * jax.random.normal(key_of[2], (LAYERS, D), jnp.float32), 0.5, 1.5)
    router_weight = normal_values(key_of[3], (LAYERS, D, EXPERTS), D ** -0.5, 0.0625, ((1, 8),))
    gate_codes = plant(jax.random.randint(key_of[4], (LAYERS, EXPERTS, D // 2, FF), 0, 256), jax.random.fold_in(key_of[4], 1), 0, 255).astype(jnp.int32)
    gate_scales = plant(jax.random.randint(key_of[5], (LAYERS, EXPERTS, D // GROUP, FF), IN_SHIFT - 1, IN_SHIFT + 2), jax.random.fold_in(key_of[5], 1), IN_SHIFT - 1, (IN_SHIFT + 2) - 1).astype(jnp.int32)
    up_codes = plant(jax.random.randint(key_of[6], (LAYERS, EXPERTS, D // 2, FF), 0, 256), jax.random.fold_in(key_of[6], 1), 0, 255).astype(jnp.int32)
    up_scales = plant(jax.random.randint(key_of[7], (LAYERS, EXPERTS, D // GROUP, FF), IN_SHIFT - 1, IN_SHIFT + 2), jax.random.fold_in(key_of[7], 1), IN_SHIFT - 1, (IN_SHIFT + 2) - 1).astype(jnp.int32)
    down_codes = plant(jax.random.randint(key_of[8], (LAYERS, EXPERTS, FF // 2, D), 0, 256), jax.random.fold_in(key_of[8], 1), 0, 255).astype(jnp.int32)
    down_scales = plant(jax.random.randint(key_of[9], (LAYERS, EXPERTS, FF // GROUP, D), OUT_SHIFT - 1, OUT_SHIFT + 2), jax.random.fold_in(key_of[9], 1), OUT_SHIFT - 1, (OUT_SHIFT + 2) - 1).astype(jnp.int32)
    return {"tokens": tokens, "routes": routes, "norm_gain": norm_gain, "router_weight": router_weight, "gate_codes": gate_codes, "gate_scales": gate_scales, "up_codes": up_codes, "up_scales": up_scales, "down_codes": down_codes, "down_scales": down_scales}


def hadamard(table_order):
    matrix = np.ones((1, 1), np.float32)
    for repeat_idx in range(table_order.bit_length() - 1):
        matrix = np.kron(np.array([[1.0, 1.0], [1.0, -1.0]], np.float32), matrix)
    return matrix

def unpack(words):
    shifts = (jnp.arange(2, dtype=jnp.int32) * 4).astype(jnp.int32)
    nibbles = jnp.bitwise_and(jnp.right_shift(words[:, None, :], shifts[None, :, None]), 15) - 8
    return nibbles.reshape(words.shape[0] * 2, words.shape[1]).astype(jnp.int32)

def dequant(words, scales):
    codes = unpack(words)
    groups = scales.shape[0]
    shaped = codes.reshape(groups, codes.shape[0] // groups, codes.shape[1]).astype(jnp.float32)
    factor = jnp.exp2(-scales.astype(jnp.float32))
    return (shaped * factor[:, None, :]).reshape(codes.shape).astype(jnp.bfloat16)

def rotate_rows(matrix_rows):
    row_count = matrix_rows.shape[0]
    local_width = D // N_TENSOR
    first_order = 1 << (local_width.bit_length() - 1) // 2
    second_order = local_width // first_order
    first_table = jnp.asarray(hadamard(first_order), jnp.float32)
    second_table = jnp.asarray(hadamard(second_order), jnp.float32)
    cross_table = jnp.asarray(hadamard(N_TENSOR), jnp.float32)
    blocks = matrix_rows.reshape(row_count, N_TENSOR, first_order, second_order).astype(jnp.float32)
    section_one = jnp.einsum('rnab,bc->rnac', blocks, second_table, precision=lax.Precision.HIGHEST)
    section_two = jnp.einsum('rnac,ad->rndc', section_one, first_table, precision=lax.Precision.HIGHEST)
    section_two = section_two.reshape(row_count, N_TENSOR, local_width)
    outer_sum = jnp.einsum('rne,nm->rme', section_two, cross_table, precision=lax.Precision.HIGHEST)
    return (outer_sum.reshape(row_count, D) * (1.0 / math.sqrt(D))).astype(jnp.bfloat16)

def reference(tokens, routes, norm_gain, router_weight, gate_codes, gate_scales, up_codes, up_scales, down_codes, down_scales):
    block_count = TOKENS // TOK_DEV
    flat_routes = routes.reshape(block_count, 2 * TOK_DEV)
    onehot = (flat_routes[:, :, None] == jnp.arange(EXPERTS, dtype=jnp.int32)[None, None, :]).astype(jnp.int32)
    earlier = jnp.cumsum(onehot, axis=1) - onehot
    ranks = lax.optimization_barrier(jnp.sum(earlier * onehot, axis=2))
    positions = (jnp.arange(block_count, dtype=jnp.int32)[:, None] * CAP + ranks).astype(jnp.int32)
    positions = positions.reshape(TOKENS, 2)
    token_ids = (jnp.arange(2 * TOKENS, dtype=jnp.int32) // 2).astype(jnp.int32)
    owner_table = jnp.full((EXPERTS, block_count * CAP), -1, jnp.int32)
    owner_table = owner_table.at[routes.reshape(-1), positions.reshape(-1)].set(token_ids)
    local_hidden = FF // N_TENSOR
    stream = tokens.astype(jnp.float32)
    for layer_idx in range(LAYERS):
        square = lax.optimization_barrier(jnp.sum(stream * stream, axis=1))
        normed = (stream * lax.rsqrt(square / D + 1e-05)[:, None] * norm_gain[layer_idx][None, :]).astype(jnp.bfloat16)
        logits = jnp.dot(normed, router_weight[layer_idx], preferred_element_type=jnp.float32)
        chosen = jnp.take_along_axis(logits, routes, axis=1)
        first_weight = jax.nn.sigmoid(chosen[:, 0] - chosen[:, 1])
        rotated = rotate_rows(normed)

        def run_expert(operands):
            slot_tokens, gate_c, gate_s, up_c, up_s, down_c, down_s = operands
            inputs = jnp.where((slot_tokens >= 0)[:, None], rotated[jnp.maximum(slot_tokens, 0)], jnp.zeros((), jnp.bfloat16))
            gate_out = jnp.dot(inputs, dequant(gate_c, gate_s), preferred_element_type=jnp.float32)
            up_out = jnp.dot(inputs, dequant(up_c, up_s), preferred_element_type=jnp.float32)
            activ = (jax.nn.silu(gate_out) * up_out).astype(jnp.bfloat16)
            slot_count = activ.shape[0]
            down_full = dequant(down_c, down_s).reshape(N_TENSOR, local_hidden, D).astype(jnp.float32)
            partials = jnp.einsum('sna,nad->snd', activ.reshape(slot_count, N_TENSOR, local_hidden).astype(jnp.float32), down_full, precision=lax.Precision.HIGHEST)
            rounded = lax.optimization_barrier(partials.astype(jnp.bfloat16)).astype(jnp.float32)
            return lax.optimization_barrier(jnp.sum(rounded, axis=1)).astype(jnp.bfloat16)
        expert_all = lax.map(run_expert, (owner_table, gate_codes[layer_idx], gate_scales[layer_idx], up_codes[layer_idx], up_scales[layer_idx], down_codes[layer_idx], down_scales[layer_idx]))
        picked = expert_all[routes, positions].astype(jnp.float32)
        stream = stream + first_weight[:, None] * picked[:, 0] + (1.0 - first_weight)[:, None] * picked[:, 1]
    return stream.astype(jnp.bfloat16)
```

```python
import functools
import math

import jax
import jax.numpy as jnp
from jax import lax
from jax.experimental import pallas as pl
from jax.experimental.pallas import tpu as pltpu
from jax.sharding import PartitionSpec as P

LAYERS = 2
TOK = 128
WIDTH = 1024
HALF = 512
CAP = 24
CHUNK = 2 * CAP
ROWS = 16 * CHUNK
GROUP = 4 * CHUNK
VIA_UP = (0, 3)
VIA_DOWN = (1, 2)
MESH = pl.DeviceIdType.MESH
F32 = jnp.float32
BF16 = jnp.bfloat16
I32 = jnp.int32


def dot(a, b):
    return jnp.dot(a, b, preferred_element_type=F32)


def back(a, b):
    return ((-a) % 4) * 4 + (-b) % 4


def iota(shape, dim):
    return lax.broadcasted_iota(I32, shape, dim)


def walsh(values):
    values = list(values)
    for bit in (1, 2, 4):
        for i in range(8):
            if not i & bit:
                low, high = values[i], values[i | bit]
                values[i], values[i | bit] = low + high, low - high
    return values


def rows_of(group):
    return pl.ds(group * GROUP, GROUP)


def kernel(
    tok_ref, routes_ref, gain_ref, rw_ref, gc_hbm, gs_ref, uc_hbm, us_ref, dc_hbm, ds_ref,
    out_ref,
    stream, had, cg, cu, cd, wp, wd, gath, pick, xr, sl, xf, acc, actx, actp,
    own, pk1, sibr, rh, rf, ret, ex, fw_ref,
    code_sem, ex_s, ex_r, disp_s, disp_r, ag_s, ag_r, rs_s, rs_r, ret_s, ret_r,
):
    e = lax.axis_index("expert")
    t = lax.axis_index("tensor")
    z, y = e // 4, e % 4
    x, c = t // 2, t % 2

    def expert_at(a, b):
        return {"expert": ((z + a) % 4) * 4 + (y + b) % 4, "tensor": t}

    def tensor_at(index):
        return {"expert": e, "tensor": index}

    sibling = tensor_at(2 * x + (1 - c))
    up = tensor_at(2 * ((x + 1) % 4) + c)
    down = tensor_at(2 * ((x + 3) % 4) + c)

    def block(d, k):
        core = c if k == 0 else 1 - c
        return 2 * ((x + d) % 4) + core

    def remote(src, dst, ssem, rsem, device):
        return pltpu.make_async_remote_copy(
            src_ref=src, dst_ref=dst, send_sem=ssem, recv_sem=rsem,
            device_id=device, device_id_type=MESH,
        )

    def code_copies(l):
        return [
            pltpu.make_async_copy(gc_hbm.at[l], cg, code_sem.at[0]),
            pltpu.make_async_copy(uc_hbm.at[l], cu, code_sem.at[1]),
            pltpu.make_async_copy(dc_hbm.at[l], cd, code_sem.at[2]),
        ]

    barrier = pltpu.get_barrier_semaphore()
    for a in range(4):
        for b in range(4):
            if a or b:
                pl.semaphore_signal(
                    barrier, inc=1, device_id=expert_at(a, b), device_id_type=MESH
                )
    for k in range(1, 8):
        pl.semaphore_signal(
            barrier, inc=1, device_id=tensor_at((t + k) % 8), device_id_type=MESH
        )

    eye = (iota((TOK, TOK), 0) == iota((TOK, TOK), 1)).astype(F32)
    below = (iota((TOK, TOK), 0) > iota((TOK, TOK), 1)).astype(BF16)
    lanes = iota((TOK, 16), 1)
    picks, rels = [], []
    for k in range(2):
        named = routes_ref[:, k : k + 1]
        picks.append((named == lanes).astype(F32))
        rels.append((((named // 4) - z + 4) % 4) * 4 + ((named % 4) - y + 4) % 4)
    earlier = dot(below, (picks[0] + picks[1]).astype(BF16))
    slots = []
    for k in range(2):
        rank = jnp.sum(picks[k] * earlier, axis=1, keepdims=True)
        slots.append(rels[k].astype(F32) * CAP + rank)
    slot_rows = [jnp.sum(eye * s, axis=0, keepdims=True).astype(I32) for s in slots]
    slot_cols = [s.astype(I32) for s in slots]
    sign = picks[0] - picks[1]

    row = iota((ROWS, 1), 0)
    chunk = row // CHUNK
    inner = row - chunk * CHUNK
    row_half = (inner >= CAP).astype(I32)
    row_slot = chunk * CAP + inner - row_half * CAP
    col_half = (iota((1, 2 * TOK), 1) >= TOK).astype(I32)
    both = [jnp.concatenate([s, s], axis=1) for s in slot_rows]
    hit = (row_half == col_half) & ((row_slot == both[0]) | (row_slot == both[1]))
    gath[...] = hit.astype(F32).astype(BF16)

    lane = iota((1, ROWS), 1)
    lane_chunk = lane // CHUNK
    lane_inner = lane - lane_chunk * CHUNK
    lane_half = (lane_inner >= CAP).astype(I32)
    lane_slot = lane_chunk * CAP + lane_inner - lane_half * CAP
    for k in range(2):
        for h in range(2):
            hit = (lane_half == h) & (lane_slot == slot_cols[k])
            pick[k, pl.ds(h * TOK, TOK), :] = hit.astype(F32).astype(BF16)

    @pl.loop(0, 32)
    def _(i):
        at = pl.multiple_of(i * 32, 32)
        r = iota((32, WIDTH), 0) + at
        j = iota((32, WIDTH), 1)
        v = r & (2 * (j & (HALF - 1)) + (j >> 9))
        v = v ^ (v >> 8)
        v = v ^ (v >> 4)
        v = v ^ (v >> 2)
        v = v ^ (v >> 1)
        had[pl.ds(at, 32), :] = (1 - 2 * (v & 1)).astype(F32).astype(BF16)

    stream[...] = tok_ref[...].astype(F32)
    for copy in code_copies(0):
        copy.start()
    pl.semaphore_wait(barrier, 22)

    def exchange(l, which, column):
        ex[l, which, 0] = jnp.broadcast_to(
            jnp.sum(eye * column, axis=0, keepdims=True), (8, TOK)
        )
        copies = [
            remote(
                ex.at[l, which, 0], ex.at[l, which, k], ex_s.at[l, which, k],
                ex_r.at[l, which, k], tensor_at((t + k) % 8),
            )
            for k in range(1, 8)
        ]
        for copy in copies:
            copy.start()
        return copies

    def exchanged(l, which, copies):
        for copy in copies:
            copy.wait_recv()
        total = ex[l, which, 0]
        for k in range(1, 8):
            total = total + ex[l, which, k]
        return jnp.sum(eye * total[0:1, :], axis=1, keepdims=True)

    def prepare_in(l, step):
        at = pl.multiple_of(step * 32, 32)
        for kind, (codes, scales) in enumerate(((cg, gs_ref), (cu, us_ref))):
            words = [codes[pl.ds(m * HALF + at, 32), :] for m in range(8)]
            shifts = [10 - scales[l, pl.ds(m * 8 + step // 2, 1), :] for m in range(8)]
            for k in range(2):
                values = walsh(
                    ((((w >> (4 * k)) & 15) - 8) << s) for w, s in zip(words, shifts)
                )
                column = k * 256 + kind * 128
                for n in range(8):
                    wp[n, pl.ds(at, 32), column : column + 128] = (
                        values[n].astype(F32).astype(BF16)
                    )

    def prepare_out(l, n):
        for h in range(2):
            at = pl.multiple_of(n * WIDTH + h * HALF, HALF)
            words = cd[:, pl.ds(at, HALF)]
            shift = 8 - ds_ref[pl.ds(l, 1), pl.ds(at, HALF)]
            for k in range(2):
                value = (((words >> (4 * k)) & 15) - 8) << shift
                wd[n, pl.ds(h * 128 + k * 64, 64), :] = (
                    value.astype(F32) * (2.0**-8)
                ).astype(BF16)

    def multiply_in(l, d, k, first=False):
        n = block(d, k)

        @pl.loop(0, 4)
        def _(g):
            at = pl.ds(pl.multiple_of(g * GROUP, GROUP), GROUP)
            value = dot(xf[l, d, k, at, :], wp[n])
            if first:
                acc[at, :] = value
            else:
                acc[at, :] += value

    def multiply_out(d, k):
        n = block(d, k)
        target = own if k == 0 else pk1

        @pl.loop(0, 4)
        def _(g):
            at = pl.ds(pl.multiple_of(g * GROUP, GROUP), GROUP)
            target[d, at, :] = dot(actp[at, :], wd[n]).astype(BF16)

    def add_into(d, g, parts):
        total = own[d, rows_of(g), :].astype(F32)
        for part in parts:
            total = total + part.astype(F32)
        own[d, rows_of(g), :] = total.astype(BF16)

    mix = (
        (iota((256, 256), 0) >> 7 == iota((256, 256), 1) >> 7)
        & (
            iota((256, 256), 1) & 127
            == ((iota((256, 256), 0) & 127) >> 1) + 64 * (iota((256, 256), 0) & 1)
        )
    ).astype(F32).astype(BF16)

    def layer(l, carry):
        sends = []
        st = stream[...]
        squares = exchange(l, 0, jnp.sum(st * st, axis=1, keepdims=True))
        sends += squares
        square = exchanged(l, 0, squares)
        normed = (
            st * lax.rsqrt(square / (8 * WIDTH) + 1e-05) * gain_ref[pl.ds(l, 1), :]
        ).astype(BF16)
        for h in range(2):
            xr[pl.ds(h * TOK, TOK), :] = dot(
                normed, had[:, h * HALF : (h + 1) * HALF]
            ).astype(BF16)

        dispatch = {}
        for a in (0, 1, 3, 2):
            value = dot(gath[rows_of(a), :], xr[...]).astype(BF16)
            sl[rows_of(a), :] = value
            if a == 0:
                xf[l, 0, 0, 0:CHUNK, :] = value[0:CHUNK, :]
            for b in range(4):
                if a or b:
                    j = back(a, b)
                    dispatch[j] = remote(
                        sl.at[pl.ds((a * 4 + b) * CHUNK, CHUNK), :],
                        xf.at[l, 0, 0, pl.ds(j * CHUNK, CHUNK), :],
                        disp_s.at[l, j], disp_r.at[l, j], expert_at(a, b),
                    )
                    dispatch[j].start()
        sends += list(dispatch.values())

        logits = dot(normed, rw_ref[l])
        shares = exchange(l, 1, jnp.sum(logits * sign, axis=1, keepdims=True))
        sends += shares

        codes = code_copies(l)
        codes[0].wait()
        codes[1].wait()

        def gather(kind, g, src, dst, device):
            return remote(
                xf.at[(l,) + src + (rows_of(g),)], xf.at[(l,) + dst + (rows_of(g),)],
                ag_s.at[l, kind, g], ag_r.at[l, kind, g], device,
            )

        to_sib, to_up, to_down = {}, {}, {}
        for i, g in enumerate((0, 3, 1, 2)):
            @pl.loop(4 * i, 4 * i + 4)
            def _(step):
                prepare_in(l, step)

            for b in range(4):
                if g or b:
                    dispatch[g * 4 + b].wait_recv()
            to_up[g] = gather(1, g, (0, 0), (3, 0), up)
            to_down[g] = gather(2, g, (0, 0), (1, 0), down)
            to_sib[g] = gather(0, g, (0, 0), (0, 1), sibling)
            to_up[g].start()
            to_down[g].start()
            to_sib[g].start()
        codes[2].wait()

        multiply_in(l, 0, 0, first=True)

        @pl.loop(0, 8)
        def _(n):
            prepare_out(l, n)

        @pl.when(l + 1 < LAYERS)
        def _():
            for copy in code_copies(l + 1):
                copy.start()

        below_sib, above_sib, two = {}, {}, {}
        for g in (0, 3, 1, 2):
            to_up[g].wait_recv()
            if g in VIA_UP:
                two[g] = gather(5, g, (3, 0), (2, 0), up)
                two[g].start()
            below_sib[g] = gather(3, g, (3, 0), (3, 1), sibling)
            below_sib[g].start()
            to_down[g].wait_recv()
            if g in VIA_DOWN:
                two[g] = gather(5, g, (1, 0), (2, 0), down)
                two[g].start()
            above_sib[g] = gather(4, g, (1, 0), (1, 1), sibling)
            above_sib[g].start()
        multiply_in(l, 3, 0)
        multiply_in(l, 1, 0)
        for g in range(4):
            to_sib[g].wait_recv()
        multiply_in(l, 0, 1)
        two_sib = {}
        for g in (0, 3, 1, 2):
            two[g].wait_recv()
            two_sib[g] = gather(6, g, (2, 0), (2, 1), sibling)
            two_sib[g].start()
        for g in range(4):
            below_sib[g].wait_recv()
        multiply_in(l, 3, 1)
        for g in range(4):
            above_sib[g].wait_recv()
        multiply_in(l, 1, 1)
        multiply_in(l, 2, 0)
        for g in range(4):
            two_sib[g].wait_recv()
        multiply_in(l, 2, 1)
        for table in (to_sib, to_up, to_down, below_sib, above_sib, two, two_sib):
            sends += list(table.values())

        factor = 2.0**-10 / math.sqrt(8 * WIDTH)
        zero = jnp.zeros((CAP, 128), F32)

        @pl.loop(0, 16)
        def _(j):
            even = pl.ds(pl.multiple_of(j * CHUNK, 8), CAP)
            odd = pl.ds(pl.multiple_of(j * CHUNK + CAP, 8), CAP)
            total = (acc[even, 0:256] + acc[odd, 256:512]) * factor
            gate, value = total[:, 0:128], total[:, 128:256]
            act = gate / (1.0 + jnp.exp(-gate)) * value
            actx[even, 0:128] = act
            actx[even, 128:256] = zero
            actx[odd, 0:128] = zero
            actx[odd, 128:256] = act

        actp[...] = dot(actx[...].astype(BF16), mix).astype(BF16)

        def scatter(kind, g, src, dst, device):
            return remote(src, dst, rs_s.at[l, kind, g], rs_r.at[l, kind, g], device)

        sib = {}

        def to_sibling(d):
            multiply_out(d, 1)
            sib[d] = scatter(0, d, pk1.at[d], sibr.at[l, d], sibling)
            sib[d].start()

        to_sibling(2)
        multiply_out(2, 0)
        to_sibling(1)
        sib[2].wait_recv()
        half, whole_up, whole_down = {}, {}, {}
        for g in (3, 2, 0, 1):
            add_into(2, g, [sibr[l, 2, rows_of(g), :]])
            half[g] = scatter(
                1, g, own.at[2, rows_of(g), :], rh.at[l, rows_of(g), :],
                up if g in VIA_UP else down,
            )
            half[g].start()
        multiply_out(1, 0)
        to_sibling(3)
        multiply_out(3, 0)

        def send_whole(d, g, parts):
            add_into(d, g, [sibr[l, d, rows_of(g), :]] + parts)
            table, kind, device = (
                (whole_up, 2, up) if d == 1 else (whole_down, 3, down)
            )
            table[g] = scatter(
                kind, g, own.at[d, rows_of(g), :], rf.at[l, kind - 2, rows_of(g), :], device
            )
            table[g].start()

        sib[1].wait_recv()
        send_whole(1, 2, [])
        send_whole(1, 1, [])
        sib[3].wait_recv()
        send_whole(3, 3, [])
        send_whole(3, 0, [])
        to_sibling(0)
        multiply_out(0, 0)
        for g in (3, 2, 0, 1):
            half[g].wait_recv()
            send_whole(1 if g in VIA_UP else 3, g, [rh[l, rows_of(g), :]])
        sib[0].wait_recv()
        returns = {}
        for g in (3, 2, 0, 1):
            whole_up[g].wait_recv()
            whole_down[g].wait_recv()
            add_into(
                0, g,
                [sibr[l, 0, rows_of(g), :], rf[l, 0, rows_of(g), :], rf[l, 1, rows_of(g), :]],
            )
            for b in range(4):
                if g or b:
                    j = back(g, b)
                    returns[j] = remote(
                        own.at[0, pl.ds((g * 4 + b) * CHUNK, CHUNK), :],
                        ret.at[l, pl.ds(j * CHUNK, CHUNK), :],
                        ret_s.at[l, j], ret_r.at[l, j], expert_at(g, b),
                    )
                    returns[j].start()
                else:
                    ret[l, 0:CHUNK, :] = own[0, 0:CHUNK, :]
        for table in (sib, half, whole_up, whole_down, returns):
            sends += list(table.values())

        diff = exchanged(l, 1, shares)
        weight = 1.0 / (1.0 + jnp.exp(-diff))
        for j in range(1, 16):
            returns[j].wait_recv()
        for h in range(2):
            part = pl.ds(h * TOK, TOK)
            first = dot(pick[0, part, :], ret[l])
            second = dot(pick[1, part, :], ret[l])
            columns = slice(h * HALF, (h + 1) * HALF)
            stream[:, columns] = (
                stream[:, columns] + weight * first + (1.0 - weight) * second
            )
        for copy in sends:
            copy.wait_send()
        return carry

    lax.fori_loop(0, LAYERS, layer, 0)
    out_ref[...] = stream[...].astype(BF16)


def per_device(
    tokens, routes, norm_gain, router_weight, gate_codes, gate_scales, up_codes, up_scales,
    down_codes, down_scales,
):
    vmem = pl.BlockSpec(memory_space=pltpu.VMEM)
    anywhere = pl.BlockSpec(memory_space=pl.ANY)
    dma = pltpu.SemaphoreType.DMA
    return pl.pallas_call(
        kernel,
        out_shape=jax.ShapeDtypeStruct((TOK, WIDTH), BF16),
        in_specs=[
            vmem, vmem, vmem, vmem, anywhere, vmem, anywhere, vmem, anywhere, vmem,
        ],
        out_specs=vmem,
        scratch_shapes=[
            pltpu.VMEM((TOK, WIDTH), F32),
            pltpu.VMEM((WIDTH, WIDTH), BF16),
            pltpu.VMEM((4096, 128), I32),
            pltpu.VMEM((4096, 128), I32),
            pltpu.VMEM((64, 8192), I32),
            pltpu.VMEM((8, HALF, HALF), BF16),
            pltpu.VMEM((8, 256, HALF), BF16),
            pltpu.VMEM((ROWS, 2 * TOK), BF16),
            pltpu.VMEM((2, 2 * TOK, ROWS), BF16),
            pltpu.VMEM((2 * TOK, HALF), BF16),
            pltpu.VMEM((ROWS, HALF), BF16),
            pltpu.VMEM((LAYERS, 4, 2, ROWS, HALF), BF16),
            pltpu.VMEM((ROWS, HALF), F32),
            pltpu.VMEM((ROWS, 256), F32),
            pltpu.VMEM((ROWS, 256), BF16),
            pltpu.VMEM((4, ROWS, HALF), BF16),
            pltpu.VMEM((4, ROWS, HALF), BF16),
            pltpu.VMEM((LAYERS, 4, ROWS, HALF), BF16),
            pltpu.VMEM((LAYERS, ROWS, HALF), BF16),
            pltpu.VMEM((LAYERS, 2, ROWS, HALF), BF16),
            pltpu.VMEM((LAYERS, ROWS, HALF), BF16),
            pltpu.VMEM((LAYERS, 2, 8, 8, TOK), F32),
            pltpu.VMEM((TOK, 128), F32),
            dma((3,)),
            dma((LAYERS, 2, 8)), dma((LAYERS, 2, 8)),
            dma((LAYERS, 16)), dma((LAYERS, 16)),
            dma((LAYERS, 7, 4)), dma((LAYERS, 7, 4)),
            dma((LAYERS, 4, 4)), dma((LAYERS, 4, 4)),
            dma((LAYERS, 16)), dma((LAYERS, 16)),
        ],
        compiler_params=pltpu.CompilerParams(
            collective_id=0, has_side_effects=True, vmem_limit_bytes=60 << 20
        ),
        name="moe_layers",
    )(
        tokens, routes, norm_gain, router_weight, gate_codes.reshape(LAYERS, 4096, 128),
        gate_scales.reshape(LAYERS, 64, 128), up_codes.reshape(LAYERS, 4096, 128),
        up_scales.reshape(LAYERS, 64, 128), down_codes.reshape(LAYERS, 64, 8192),
        down_scales.reshape(LAYERS, 8192),
    )


def solution(mesh):
    in_specs = (
        P("expert", "tensor"),
        P("expert", None),
        P(None, "tensor"),
        P(None, "tensor", None),
        P(None, "expert", None, "tensor"),
        P(None, "expert", None, "tensor"),
        P(None, "expert", None, "tensor"),
        P(None, "expert", None, "tensor"),
        P(None, "expert", "tensor", None),
        P(None, "expert", "tensor", None),
    )
    return jax.shard_map(
        per_device, mesh=mesh, in_specs=in_specs, out_specs=P("expert", "tensor"),
        check_vma=False,
    )
```

```python
import functools
import math

import jax
import jax.numpy as jnp
from jax import lax
from jax.experimental import pallas as pl
from jax.experimental.pallas import tpu as pltpu
from jax.sharding import PartitionSpec as P

LAYERS = 2
TOK = 128
WIDTH = 1024
HALF = 512
CAP = 24
CHUNK = 2 * CAP
ROWS = 16 * CHUNK
GROUP = 4 * CHUNK
PART = 2 * GROUP
MESH = pl.DeviceIdType.MESH
F32 = jnp.float32
BF16 = jnp.bfloat16
I32 = jnp.int32


def dot(a, b):
    return jnp.dot(a, b, preferred_element_type=F32)


def place(z, y):
    return lax.rem(z + y, 2) * 8 + z * 2 + lax.div(y, 2)


def chunk_at(index):
    return pl.ds(pl.multiple_of(index * CHUNK, CHUNK), CHUNK)


def iota(shape, dim):
    return lax.broadcasted_iota(I32, shape, dim)


def walsh(values):
    values = list(values)
    for bit in (1, 2, 4):
        for i in range(8):
            if not i & bit:
                low, high = values[i], values[i | bit]
                values[i], values[i | bit] = low + high, low - high
    return values


def rows_of(group, count=1):
    return pl.ds(group * GROUP, count * GROUP)


def kernel(
    tok_ref, routes_ref, gain_ref, rw_ref, gc_hbm, gs_ref, uc_hbm, us_ref, dc_hbm, ds_ref,
    out_ref,
    stream, had, cg, cu, cd, wp, wd, gath, pick, xr, sl, xf, acc, actx, actp,
    own, pk1, sibr, rh, rf, ret, ex, weights, scale_out, scales,
    code_sem, ex_s, ex_r, scale_s, scale_r, disp_s, disp_r, ag_s, ag_r, rs_s, rs_r, ret_s, ret_r,
):
    e = lax.axis_index("expert")
    t = lax.axis_index("tensor")
    z, y = lax.div(e, 4), lax.rem(e, 4)
    x, c = lax.div(t, 2), lax.rem(t, 2)
    zs = [z] + [lax.rem(z + a, 4) for a in range(1, 4)]
    ys = [y] + [lax.rem(y + b, 4) for b in range(1, 4)]
    parity = lax.rem(z + y, 2)
    mine = place(z, y)
    xs = [x * 2] + [lax.rem(x + d, 4) * 2 for d in range(1, 4)]
    cores = [c, 1 - c]

    def expert_at(a, b):
        return {"expert": zs[a] * 4 + ys[b], "tensor": t}

    def tensor_at(index):
        return {"expert": e, "tensor": index}

    def block(d, k):
        return xs[d] + cores[k]

    sibling = tensor_at(block(0, 1))
    up = tensor_at(block(1, 0))
    down = tensor_at(block(3, 0))
    others = [tensor_at(lax.rem(t + k, 8)) for k in range(1, 8)]

    def remote(src, dst, ssem, rsem, device):
        return pltpu.make_async_remote_copy(
            src_ref=src, dst_ref=dst, send_sem=ssem, recv_sem=rsem,
            device_id=device, device_id_type=MESH,
        )

    def code_copies(l):
        return [
            pltpu.make_async_copy(gc_hbm.at[l], cg, code_sem.at[0]),
            pltpu.make_async_copy(uc_hbm.at[l], cu, code_sem.at[1]),
            pltpu.make_async_copy(dc_hbm.at[l], cd, code_sem.at[2]),
        ]

    barrier = pltpu.get_barrier_semaphore()
    for a in range(4):
        for b in range(4):
            if a or b:
                pl.semaphore_signal(
                    barrier, inc=1, device_id=expert_at(a, b), device_id_type=MESH
                )
    for other in others:
        pl.semaphore_signal(barrier, inc=1, device_id=other, device_id_type=MESH)

    for copy in code_copies(0):
        copy.start()
    eye = (iota((TOK, TOK), 0) == iota((TOK, TOK), 1)).astype(F32)
    stream[...] = tok_ref[...].astype(F32)

    def exchange_copies(l):
        return [
            remote(ex.at[l, 0], ex.at[l, k], ex_s.at[l], ex_r.at[l], others[k - 1])
            for k in range(1, 8)
        ]

    def all_of_exchange(l):
        seven = ex.at[l, pl.ds(1, 7)]
        return remote(seven, seven, ex_s.at[l], ex_r.at[l], sibling)

    def as_row(column):
        return jnp.sum(eye * column, axis=0, keepdims=True)

    def as_column(row):
        return jnp.sum(eye * row, axis=1, keepdims=True)

    below = (iota((TOK, TOK), 0) > iota((TOK, TOK), 1)).astype(BF16)
    lanes = iota((TOK, 16), 1)
    picks, rels = [], []
    for k in range(2):
        named = jnp.sum(
            eye * routes_ref[k : k + 1, :].astype(F32), axis=1, keepdims=True
        ).astype(I32)
        picks.append((named == lanes).astype(F32))
        to_z, to_y = named >> 2, named & 3
        rels.append(((to_z + to_y) & 1) * 8 + to_z * 2 + (to_y >> 1))
    earlier = dot(below, (picks[0] + picks[1]).astype(BF16))
    slots = []
    for k in range(2):
        rank = jnp.sum(picks[k] * earlier, axis=1, keepdims=True)
        slots.append(rels[k].astype(F32) * CAP + rank)
    slot_rows = [as_row(s).astype(I32) for s in slots]
    slot_cols = [s.astype(I32) for s in slots]
    sign = picks[0] - picks[1]

    row = iota((ROWS, 1), 0)
    chunk = row // CHUNK
    inner = row - chunk * CHUNK
    row_half = (inner >= CAP).astype(I32)
    row_slot = chunk * CAP + inner - row_half * CAP
    col_half = (iota((1, 2 * TOK), 1) >= TOK).astype(I32)
    both = [jnp.concatenate([s, s], axis=1) for s in slot_rows]
    hit = (row_half == col_half) & ((row_slot == both[0]) | (row_slot == both[1]))
    gath[...] = hit.astype(F32).astype(BF16)

    @pl.loop(0, 32)
    def _(i):
        at = pl.multiple_of(i * 32, 32)
        r = iota((32, WIDTH), 0) + at
        j = iota((32, WIDTH), 1)
        v = r & (2 * (j & (HALF - 1)) + (j >> 9))
        v = v ^ (v >> 8)
        v = v ^ (v >> 4)
        v = v ^ (v >> 2)
        v = v ^ (v >> 1)
        had[pl.ds(at, 32), :] = (1 - 2 * (v & 1)).astype(F32).astype(BF16)

    def prepare_in(l, step):
        at = pl.multiple_of(step * 32, 32)
        for kind, (codes, scales) in enumerate(((cg, gs_ref), (cu, us_ref))):
            words = [codes[pl.ds(m * HALF + at, 32), :] for m in range(8)]
            shifts = [10 - scales[l, pl.ds(m * 8 + step // 2, 1), :] for m in range(8)]
            for k in range(2):
                values = walsh(
                    ((((w >> (4 * k)) & 15) - 8) << s) for w, s in zip(words, shifts)
                )
                column = k * 256 + kind * 128
                for n in range(8):
                    wp[n, pl.ds(at, 32), column : column + 128] = (
                        values[n].astype(F32).astype(BF16)
                    )

    def prepare_out(l, n):
        for h in range(2):
            at = pl.multiple_of(n * WIDTH + h * HALF, HALF)
            words = cd[:, pl.ds(at, HALF)]
            shift = 8 - ds_ref[l, :, pl.ds(at, HALF)]
            for k in range(2):
                value = (((words >> (4 * k)) & 15) - 8) << shift
                wd[n, pl.ds(h * 128 + k * 64, 64), :] = (
                    value.astype(F32) * (2.0**-8)
                ).astype(BF16)

    def multiply_in(l, s, d, k, first=False):
        n = block(d, k)

        @pl.loop(0, 2)
        def _(i):
            at = pl.ds(pl.multiple_of(i * GROUP, GROUP), GROUP)
            rows = pl.ds(pl.multiple_of((2 * s + i) * GROUP, GROUP), GROUP)
            value = dot(xf[l, d, k, rows, :], wp[n])
            if first:
                acc[at, :] = value
            else:
                acc[at, :] += value

    def multiply_out(s, d, k):
        n = block(d, k)
        target = own if k == 0 else pk1

        @pl.loop(2 * s, 2 * s + 2)
        def _(g):
            at = pl.ds(pl.multiple_of(g * GROUP, GROUP), GROUP)
            target[d, at, :] = dot(actp[at, :], wd[n]).astype(BF16)

    def add_into(d, rows, parts):
        total = own[d, rows, :].astype(F32)
        for part in parts:
            total = total + part[rows, :].astype(F32)
        own[d, rows, :] = total.astype(BF16)

    mix = (
        (iota((256, 256), 0) >> 7 == iota((256, 256), 1) >> 7)
        & (
            iota((256, 256), 1) & 127
            == ((iota((256, 256), 0) & 127) >> 1) + 64 * (iota((256, 256), 0) & 1)
        )
    ).astype(F32).astype(BF16)

    hops = sorted(
        ((a, b) for a in range(4) for b in range(4) if a or b),
        key=lambda ab: -(min(ab[0], 4 - ab[0]) + min(ab[1], 4 - ab[1])),
    )
    targets = [(expert_at(a, b), place(zs[a], ys[b])) for a, b in hops]
    rest = pl.ds(CHUNK, ROWS - CHUNK)

    def dispatch_sent(l):
        remote(
            sl.at[rest, :], xf.at[l, 0, 0, rest, :], disp_s.at[l], disp_r.at[l, 0], sibling
        ).wait_send()

    def slot_values(l):
        gained = (stream[...] * gain_ref[pl.ds(l, 1), :]).astype(BF16)
        for h in range(2):
            xr[pl.ds(h * TOK, TOK), :] = dot(
                gained, had[:, h * HALF : (h + 1) * HALF]
            ).astype(BF16)

        @pl.loop(0, 4)
        def _(p):
            at = pl.ds(pl.multiple_of(p * GROUP, GROUP), GROUP)
            sl[at, :] = dot(gath[at, :], xr[...]).astype(BF16)

        return gained

    def send_slots(l, gained):
        group = lax.div(mine, 4)
        for device, index in targets:
            remote(
                sl.at[chunk_at(index), :], xf.at[l, 0, 0, chunk_at(mine), :],
                disp_s.at[l], disp_r.at[l, group], device,
            ).start()
        pltpu.make_async_copy(
            sl.at[chunk_at(mine), :], xf.at[l, 0, 0, chunk_at(mine), :], disp_r.at[l, group]
        ).start()
        st = stream[...]
        squares = jnp.sum(st * st, axis=1, keepdims=True)
        logits = lax.dot_general(
            gained, rw_ref[l], (((1,), (1,)), ((), ())), preferred_element_type=F32
        )
        diff = jnp.sum(logits * sign, axis=1, keepdims=True)
        ex[l, 0] = jnp.where(iota((8, TOK), 0) == 0, as_row(squares), as_row(diff))
        for copy in exchange_copies(l):
            copy.start()

    def send_scales(l):
        all_of_exchange(l).wait_recv()
        total = ex[l, 0]
        for k in range(1, 8):
            total = total + ex[l, k]
        factor = lax.rsqrt(as_column(total[0:1, :]) / (8 * WIDTH) + 1e-05)
        weights[...] = 1.0 / (1.0 + jnp.exp(-factor * as_column(total[1:2, :])))
        at = iota((TOK, TOK), 1)
        for p in range(4):
            slot = (p * 4 + (at >> 5)) * CAP + (at & 31)
            hit = ((slot == slot_cols[0]) | (slot == slot_cols[1])) & ((at & 31) < CAP)
            row = jnp.sum(jnp.where(hit, factor, 0.0), axis=0, keepdims=True)
            scale_out[l, p] = jnp.broadcast_to(row, (8, TOK))
        for device, index in targets:
            remote(
                scale_out.at[l, lax.div(index, 4)], scales.at[l, mine], scale_s.at[l],
                scale_r.at[l, parity], device,
            ).start()
        pltpu.make_async_copy(
            scale_out.at[l, lax.div(mine, 4)], scales.at[l, mine], scale_r.at[l, parity]
        ).start()

    def combine(l):
        weight = weights[...]
        pltpu.make_async_copy(own.at[0], ret.at[l], ret_r.at[l]).wait()
        for h in range(2):
            part = pl.ds(h * TOK, TOK)
            first = dot(pick[0, part, :], ret[l])
            second = dot(pick[1, part, :], ret[l])
            columns = slice(h * HALF, (h + 1) * HALF)
            stream[:, columns] = (
                stream[:, columns] + weight * first + (1.0 - weight) * second
            )

    def prepare(l):
        codes = code_copies(l)
        for copy in codes:
            copy.wait()

        @pl.loop(0, 16)
        def _(step):
            prepare_in(l, step)

        @pl.loop(0, 8)
        def _(n):
            prepare_out(l, n)

        @pl.when(l + 1 < LAYERS)
        def _():
            for copy in code_copies(l + 1):
                copy.start()

    def gather(l, kind, part, rows, src, dst, device):
        return remote(
            xf.at[(l,) + src + (rows,)], xf.at[(l,) + dst + (rows,)],
            ag_s.at[l, kind], ag_r.at[l, kind, part], device,
        )

    def up_copy(l, g):
        return gather(l, 1, g, rows_of(g), (0, 0), (3, 0), up)

    def down_copy(l, g):
        return gather(l, 2, g, rows_of(g), (0, 0), (1, 0), down)

    def two_copy(l, g):
        if g % 2 == 0:
            return gather(l, 5, g, rows_of(g), (3, 0), (2, 0), up)
        return gather(l, 6, g, rows_of(g), (1, 0), (2, 0), down)

    def two_sib_copy(l, g):
        return gather(l, 7 + g % 2, g, rows_of(g), (2, 0), (2, 1), sibling)

    def sib_copy(l, s, kind, d):
        return gather(l, kind, s, rows_of(2 * s, 2), (d, 0), (d, 1), sibling)

    def send_own(l, s):
        even, odd = 2 * s, 2 * s + 1
        for g in (even, odd):
            arrived = xf.at[l, 0, 0, rows_of(g), :]
            pltpu.make_async_copy(arrived, arrived, disp_r.at[l, g]).wait()
        up_copy(l, even).start()
        down_copy(l, odd).start()
        up_copy(l, odd).start()
        down_copy(l, even).start()
        sib_copy(l, s, 0, 0).start()

    def forward(l, s):
        even, odd = 2 * s, 2 * s + 1
        up_copy(l, even).wait_recv()
        two_copy(l, even).start()
        down_copy(l, odd).wait_recv()
        two_copy(l, odd).start()
        up_copy(l, odd).wait_recv()
        sib_copy(l, s, 3, 3).start()
        down_copy(l, even).wait_recv()
        sib_copy(l, s, 4, 1).start()

    factor = 2.0**-10 / math.sqrt(8 * WIDTH)

    def hidden(l, s):
        even, odd = 2 * s, 2 * s + 1
        multiply_in(l, s, 0, 0, first=True)
        sib_copy(l, s, 0, 0).wait_recv()
        multiply_in(l, s, 0, 1)
        multiply_in(l, s, 3, 0)
        multiply_in(l, s, 1, 0)
        sib_copy(l, s, 3, 3).wait_recv()
        multiply_in(l, s, 3, 1)
        sib_copy(l, s, 4, 1).wait_recv()
        multiply_in(l, s, 1, 1)
        for g in (even, odd):
            two_copy(l, g).wait_recv()
            two_sib_copy(l, g).start()
        multiply_in(l, s, 2, 0)
        for g in (even, odd):
            two_sib_copy(l, g).wait_recv()
        multiply_in(l, s, 2, 1)

        eight = scales.at[l, pl.ds(8 * s, 8)]
        pltpu.make_async_copy(eight, eight, scale_r.at[l, s]).wait()
        lanes_of = iota((CAP, TOK), 1) == iota((CAP, TOK), 0) + lax.rem(mine, 4) * 32

        zero = jnp.zeros((CAP, 128), F32)

        @pl.loop(0, 8)
        def _(j):
            first = pl.ds(pl.multiple_of(j * CHUNK, 8), CAP)
            second = pl.ds(pl.multiple_of(j * CHUNK + CAP, 8), CAP)
            scale = jnp.sum(
                jnp.where(lanes_of, scales[l, 8 * s + j, 0:1, :], 0.0), axis=1, keepdims=True
            )
            total = (acc[first, 0:256] + acc[second, 256:512]) * (factor * scale)
            gate, value = total[:, 0:128], total[:, 128:256]
            act = gate / (1.0 + jnp.exp(-gate)) * value
            actx[first, 0:128] = act
            actx[first, 128:256] = zero
            actx[second, 0:128] = zero
            actx[second, 128:256] = act

        actp[rows_of(2 * s, 2), :] = dot(actx[...].astype(BF16), mix).astype(BF16)

    def sum_sib(l, s, d):
        rows = rows_of(2 * s, 2)
        return remote(
            pk1.at[d, rows, :], sibr.at[l, d, rows, :], rs_s.at[l, 0],
            rs_r.at[l, 0, 4 * s + d], sibling,
        )

    def sum_half(l, g):
        kind = 1 + g % 2
        return remote(
            own.at[2, rows_of(g), :], rh.at[l, rows_of(g), :], rs_s.at[l, kind],
            rs_r.at[l, kind, g], (up, down)[g % 2],
        )

    def sum_owner(l, d, g):
        kind = 3 if d == 1 else 4
        return remote(
            own.at[d, rows_of(g), :], rf.at[l, kind - 3, rows_of(g), :], rs_s.at[l, kind],
            rs_r.at[l, kind, g], up if d == 1 else down,
        )

    def to_sibling(l, s, d):
        multiply_out(s, d, 1)
        sum_sib(l, s, d).start()

    def to_owner(l, d, g, parts):
        add_into(d, rows_of(g), [sibr.at[l, d]] + parts)
        sum_owner(l, d, g).start()

    def sums_start(l, s):
        to_sibling(l, s, 2)
        multiply_out(s, 2, 0)
        to_sibling(l, s, 1)

    def sums_send(l, s):
        even, odd = 2 * s, 2 * s + 1
        sum_sib(l, s, 2).wait_recv()
        for g in (even, odd):
            add_into(2, rows_of(g), [sibr.at[l, 2]])
            sum_half(l, g).start()
        multiply_out(s, 1, 0)
        to_sibling(l, s, 3)
        sum_sib(l, s, 1).wait_recv()
        to_owner(l, 1, odd, [])
        multiply_out(s, 3, 0)
        sum_sib(l, s, 3).wait_recv()
        to_owner(l, 3, even, [])
        to_sibling(l, s, 0)
        multiply_out(s, 0, 0)

    def sums_pass(l, s):
        even, odd = 2 * s, 2 * s + 1
        sum_half(l, even).wait_recv()
        to_owner(l, 1, even, [rh.at[l]])
        sum_half(l, odd).wait_recv()
        to_owner(l, 3, odd, [rh.at[l]])

    def give_back(l, s):
        sum_sib(l, s, 0).wait_recv()
        for g in (2 * s, 2 * s + 1):
            sum_owner(l, 1, g).wait_recv()
            sum_owner(l, 3, g).wait_recv()
            add_into(0, rows_of(g), [sibr.at[l, 0], rf.at[l, 0], rf.at[l, 1]])
            for q in range(4):
                to_z = 2 * (g % 2) + q // 2
                to_y = 2 * (q % 2) + (s + to_z) % 2
                src = own.at[0, pl.ds((g * 4 + q) * CHUNK, CHUNK), :]
                dst = ret.at[l, chunk_at(mine), :]
                here = e == to_z * 4 + to_y

                @pl.when(here)
                def _():
                    pltpu.make_async_copy(src, dst, ret_r.at[l]).start()

                @pl.when(jnp.logical_not(here))
                def _():
                    remote(
                        src, dst, ret_s.at[l], ret_r.at[l],
                        {"expert": to_z * 4 + to_y, "tensor": t},
                    ).start()

    def all_sent(l):
        all_of_exchange(l).wait_send()
        fifteen = scales.at[l, pl.ds(0, 15)]
        remote(fifteen, fifteen, scale_s.at[l], scale_r.at[l, 0], sibling).wait_send()
        for kind in range(9):
            rows = pl.ds(0, ROWS if kind < 5 else PART)
            gather(l, kind, 0, rows, (0, 0), (0, 0), sibling).wait_send()
        remote(pk1, sibr.at[l], rs_s.at[l, 0], rs_r.at[l, 0, 0], sibling).wait_send()
        for kind in range(1, 5):
            rows = pl.ds(0, PART if kind < 3 else ROWS)
            remote(
                own.at[1, rows, :], rh.at[l, rows, :], rs_s.at[l, kind], rs_r.at[l, kind, 0],
                sibling,
            ).wait_send()
        remote(
            own.at[0, rest, :], ret.at[l, rest, :], ret_s.at[l], ret_r.at[l], sibling
        ).wait_send()

    def finish(l):
        combine(l)

        @pl.when(l + 1 < LAYERS)
        def _():
            dispatch_sent(l)
            send_slots(l + 1, slot_values(l + 1))

    def layer(l, carry):
        @pl.when((l > 0) & (parity == 0))
        def _():
            send_scales(l)

        send_own(l, 0)

        @pl.when((l > 0) & (parity == 1))
        def _():
            finish(l - 1)

        @pl.when(l == 0)
        def _():
            send_own(0, 1)
            send_scales(0)
            prepare(0)

        forward(l, 0)

        @pl.when((l > 0) & (parity == 1))
        def _():
            send_scales(l)

        @pl.when(l > 0)
        def _():
            send_own(l, 1)

        hidden(l, 0)

        @pl.when(l > 0)
        def _():
            all_sent(l - 1)

        sums_start(l, 0)
        forward(l, 1)
        sums_send(l, 0)
        hidden(l, 1)
        sums_start(l, 1)
        sums_pass(l, 0)
        sums_send(l, 1)

        @pl.when(l + 1 < LAYERS)
        def _():
            prepare(l + 1)

        give_back(l, 0)
        sums_pass(l, 1)

        @pl.when(parity == 0)
        def _():
            finish(l)

        give_back(l, 1)
        return carry

    gained = slot_values(0)
    pl.semaphore_wait(barrier, 22)
    send_slots(0, gained)
    lane = iota((1, ROWS), 1)
    lane_chunk = lane // CHUNK
    lane_inner = lane - lane_chunk * CHUNK
    lane_half = (lane_inner >= CAP).astype(I32)
    lane_slot = lane_chunk * CAP + lane_inner - lane_half * CAP
    for k in range(2):
        for h in range(2):
            hit = (lane_half == h) & (lane_slot == slot_cols[k])
            pick[k, pl.ds(h * TOK, TOK), :] = hit.astype(F32).astype(BF16)

    lax.fori_loop(0, LAYERS, layer, 0)

    @pl.when(parity == 1)
    def _():
        combine(LAYERS - 1)

    dispatch_sent(LAYERS - 1)
    all_sent(LAYERS - 1)
    out_ref[...] = stream[...].astype(BF16)


def per_device(
    tokens, routes, norm_gain, router_weight, gate_codes, gate_scales, up_codes, up_scales,
    down_codes, down_scales,
):
    vmem = pl.BlockSpec(memory_space=pltpu.VMEM)
    anywhere = pl.BlockSpec(memory_space=pl.ANY)
    dma = pltpu.SemaphoreType.DMA
    return pl.pallas_call(
        kernel,
        out_shape=jax.ShapeDtypeStruct((TOK, WIDTH), BF16),
        in_specs=[
            vmem, vmem, vmem, vmem, anywhere, vmem, anywhere, vmem, anywhere, vmem,
        ],
        out_specs=vmem,
        scratch_shapes=[
            pltpu.VMEM((TOK, WIDTH), F32),
            pltpu.VMEM((WIDTH, WIDTH), BF16),
            pltpu.VMEM((4096, 128), I32),
            pltpu.VMEM((4096, 128), I32),
            pltpu.VMEM((64, 8192), I32),
            pltpu.VMEM((8, HALF, HALF), BF16),
            pltpu.VMEM((8, 256, HALF), BF16),
            pltpu.VMEM((ROWS, 2 * TOK), BF16),
            pltpu.VMEM((2, 2 * TOK, ROWS), BF16),
            pltpu.VMEM((2 * TOK, HALF), BF16),
            pltpu.VMEM((ROWS, HALF), BF16),
            pltpu.VMEM((LAYERS, 4, 2, ROWS, HALF), BF16),
            pltpu.VMEM((PART, HALF), F32),
            pltpu.VMEM((PART, 256), F32),
            pltpu.VMEM((ROWS, 256), BF16),
            pltpu.VMEM((4, ROWS, HALF), BF16),
            pltpu.VMEM((4, ROWS, HALF), BF16),
            pltpu.VMEM((LAYERS, 4, ROWS, HALF), BF16),
            pltpu.VMEM((LAYERS, ROWS, HALF), BF16),
            pltpu.VMEM((LAYERS, 2, ROWS, HALF), BF16),
            pltpu.VMEM((LAYERS, ROWS, HALF), BF16),
            pltpu.VMEM((LAYERS, 8, 8, TOK), F32),
            pltpu.VMEM((TOK, 1), F32),
            pltpu.VMEM((LAYERS, 4, 8, TOK), F32),
            pltpu.VMEM((LAYERS, 16, 8, TOK), F32),
            dma((3,)),
            dma((LAYERS,)), dma((LAYERS,)),
            dma((LAYERS,)), dma((LAYERS, 2)),
            dma((LAYERS,)), dma((LAYERS, 4)),
            dma((LAYERS, 9)), dma((LAYERS, 9, 4)),
            dma((LAYERS, 5)), dma((LAYERS, 5, 8)),
            dma((LAYERS,)), dma((LAYERS,)),
        ],
        compiler_params=pltpu.CompilerParams(
            collective_id=0, has_side_effects=True, vmem_limit_bytes=60 << 20
        ),
        name="moe_layers",
    )(
        tokens, routes.T, norm_gain, router_weight.transpose(0, 2, 1),
        gate_codes.reshape(LAYERS, 4096, 128),
        gate_scales.reshape(LAYERS, 64, 128), up_codes.reshape(LAYERS, 4096, 128),
        up_scales.reshape(LAYERS, 64, 128), down_codes.reshape(LAYERS, 64, 8192),
        down_scales.reshape(LAYERS, 1, 8192),
    )


def solution(mesh):
    in_specs = (
        P("expert", "tensor"),
        P("expert", None),
        P(None, "tensor"),
        P(None, "tensor", None),
        P(None, "expert", None, "tensor"),
        P(None, "expert", None, "tensor"),
        P(None, "expert", None, "tensor"),
        P(None, "expert", None, "tensor"),
        P(None, "expert", "tensor", None),
        P(None, "expert", "tensor", None),
    )
    return jax.shard_map(
        per_device, mesh=mesh, in_specs=in_specs, out_specs=P("expert", "tensor"),
        check_vma=False,
    )
```

```python
import functools
import math

import jax
import jax.numpy as jnp
from jax import lax
from jax.experimental import pallas as pl
from jax.experimental.pallas import tpu as pltpu
from jax.sharding import PartitionSpec as P

LAYERS = 2
TOK = 128
WIDTH = 1024
HALF = 512
CAP = 24
CHUNK = 2 * CAP
ROWS = 16 * CHUNK
GROUP = 4 * CHUNK
PART = 2 * GROUP
MESH = pl.DeviceIdType.MESH
F32 = jnp.float32
BF16 = jnp.bfloat16
I32 = jnp.int32


def dot(a, b):
    return jnp.dot(a, b, preferred_element_type=F32)


def place(z, y):
    return lax.rem(z + y, 2) * 8 + z * 2 + lax.div(y, 2)


def chunk_at(index):
    return pl.ds(pl.multiple_of(index * CHUNK, CHUNK), CHUNK)


def iota(shape, dim):
    return lax.broadcasted_iota(I32, shape, dim)


def walsh(values):
    values = list(values)
    for bit in (1, 2, 4):
        for i in range(8):
            if not i & bit:
                low, high = values[i], values[i | bit]
                values[i], values[i | bit] = low + high, low - high
    return values


def rows_of(group, count=1):
    return pl.ds(group * GROUP, count * GROUP)


def kernel(
    tok_ref, routes_ref, gain_ref, rw_ref, gc_hbm, gs_ref, uc_hbm, us_ref, dc_hbm, ds_ref,
    out_ref,
    stream, had, cg, cu, cd, wp, wd, gath, pick, xr, sl, xf, acc, actx, actp,
    own, pk1, sibr, rf, ret, far_xr, far_sl, far_sum, far_in, ex, weights, scale_out, scales,
    code_sem, ex_s, ex_r, scale_s, scale_r, disp_s, disp_r, ag_s, ag_r, rs_s, rs_r, ret_s, ret_r, relay_s, relay_r,
):
    e = lax.axis_index("expert")
    t = lax.axis_index("tensor")
    z, y = lax.div(e, 4), lax.rem(e, 4)
    x, c = lax.div(t, 2), lax.rem(t, 2)
    zs = [z] + [lax.rem(z + a, 4) for a in range(1, 4)]
    ys = [y] + [lax.rem(y + b, 4) for b in range(1, 4)]
    parity = lax.rem(z + y, 2)
    mine = place(z, y)
    xs = [x * 2] + [lax.rem(x + d, 4) * 2 for d in range(1, 4)]
    cores = [c, 1 - c]

    def expert_at(a, b):
        return {"expert": zs[a] * 4 + ys[b], "tensor": t}

    def tensor_at(index):
        return {"expert": e, "tensor": index}

    def block(d, k):
        return xs[d] + cores[k]

    sibling = tensor_at(block(0, 1))
    up = tensor_at(block(1, 0))
    down = tensor_at(block(3, 0))
    across = tensor_at(block(2, 0))
    others = [tensor_at(lax.rem(t + k, 8)) for k in range(1, 8)]

    def remote(src, dst, ssem, rsem, device):
        return pltpu.make_async_remote_copy(
            src_ref=src, dst_ref=dst, send_sem=ssem, recv_sem=rsem,
            device_id=device, device_id_type=MESH,
        )

    def code_copies(l):
        return [
            pltpu.make_async_copy(gc_hbm.at[l], cg, code_sem.at[0]),
            pltpu.make_async_copy(uc_hbm.at[l], cu, code_sem.at[1]),
            pltpu.make_async_copy(dc_hbm.at[l], cd, code_sem.at[2]),
        ]

    barrier = pltpu.get_barrier_semaphore()
    for a in range(4):
        for b in range(4):
            if a or b:
                pl.semaphore_signal(
                    barrier, inc=1, device_id=expert_at(a, b), device_id_type=MESH
                )
    for other in others:
        pl.semaphore_signal(barrier, inc=1, device_id=other, device_id_type=MESH)

    for copy in code_copies(0):
        copy.start()
    eye = (iota((TOK, TOK), 0) == iota((TOK, TOK), 1)).astype(F32)
    stream[...] = tok_ref[...].astype(F32)

    def exchange_copies(l):
        return [
            remote(ex.at[l, 0], ex.at[l, k], ex_s.at[l], ex_r.at[l], others[k - 1])
            for k in range(1, 8)
        ]

    def all_of_exchange(l):
        seven = ex.at[l, pl.ds(1, 7)]
        return remote(seven, seven, ex_s.at[l], ex_r.at[l], sibling)

    def as_row(column):
        return jnp.sum(eye * column, axis=0, keepdims=True)

    def as_column(row):
        return jnp.sum(eye * row, axis=1, keepdims=True)

    below = (iota((TOK, TOK), 0) > iota((TOK, TOK), 1)).astype(BF16)
    lanes = iota((TOK, 16), 1)
    picks, rels = [], []
    for k in range(2):
        named = jnp.sum(
            eye * routes_ref[k : k + 1, :].astype(F32), axis=1, keepdims=True
        ).astype(I32)
        picks.append((named == lanes).astype(F32))
        to_z, to_y = named >> 2, named & 3
        rels.append(((to_z + to_y) & 1) * 8 + to_z * 2 + (to_y >> 1))
    earlier = dot(below, (picks[0] + picks[1]).astype(BF16))
    slots = []
    for k in range(2):
        rank = jnp.sum(picks[k] * earlier, axis=1, keepdims=True)
        slots.append(rels[k].astype(F32) * CAP + rank)
    slot_rows = [as_row(s).astype(I32) for s in slots]
    slot_cols = [s.astype(I32) for s in slots]
    sign = picks[0] - picks[1]

    row = iota((ROWS, 1), 0)
    chunk = row // CHUNK
    inner = row - chunk * CHUNK
    row_half = (inner >= CAP).astype(I32)
    row_slot = chunk * CAP + inner - row_half * CAP
    col_half = (iota((1, 2 * TOK), 1) >= TOK).astype(I32)
    both = [jnp.concatenate([s, s], axis=1) for s in slot_rows]
    hit = (row_half == col_half) & ((row_slot == both[0]) | (row_slot == both[1]))
    gath[...] = hit.astype(F32).astype(BF16)

    @pl.loop(0, 32)
    def _(i):
        at = pl.multiple_of(i * 32, 32)
        r = iota((32, WIDTH), 0) + at
        j = iota((32, WIDTH), 1)
        v = r & (2 * (j & (HALF - 1)) + (j >> 9))
        v = v ^ (v >> 8)
        v = v ^ (v >> 4)
        v = v ^ (v >> 2)
        v = v ^ (v >> 1)
        had[pl.ds(at, 32), :] = (1 - 2 * (v & 1)).astype(F32).astype(BF16)

    def prepare_in(l, step):
        at = pl.multiple_of(step * 32, 32)
        for kind, (codes, scales) in enumerate(((cg, gs_ref), (cu, us_ref))):
            words = [codes[pl.ds(m * HALF + at, 32), :] for m in range(8)]
            shifts = [10 - scales[l, pl.ds(m * 8 + step // 2, 1), :] for m in range(8)]
            for k in range(2):
                values = walsh(
                    ((((w >> (4 * k)) & 15) - 8) << s) for w, s in zip(words, shifts)
                )
                column = k * 256 + kind * 128
                for n in range(8):
                    wp[n, pl.ds(at, 32), column : column + 128] = (
                        values[n].astype(F32).astype(BF16)
                    )

    def prepare_out(l, n):
        for h in range(2):
            at = pl.multiple_of(n * WIDTH + h * HALF, HALF)
            words = cd[:, pl.ds(at, HALF)]
            shift = 8 - ds_ref[l, :, pl.ds(at, HALF)]
            for k in range(2):
                value = (((words >> (4 * k)) & 15) - 8) << shift
                wd[n, pl.ds(h * 128 + k * 64, 64), :] = (
                    value.astype(F32) * (2.0**-8)
                ).astype(BF16)

    def multiply_in(l, s, d, k, first=False):
        n = block(d, k)

        @pl.loop(0, 2)
        def _(i):
            at = pl.ds(pl.multiple_of(i * GROUP, GROUP), GROUP)
            rows = pl.ds(pl.multiple_of((2 * s + i) * GROUP, GROUP), GROUP)
            value = dot(xf[l, d, k, rows, :], wp[n])
            if first:
                acc[at, :] = value
            else:
                acc[at, :] += value

    def multiply_out(s, d, k):
        n = block(d, k)
        target = own if k == 0 else pk1

        @pl.loop(2 * s, 2 * s + 2)
        def _(g):
            at = pl.ds(pl.multiple_of(g * GROUP, GROUP), GROUP)
            target[d, at, :] = dot(actp[at, :], wd[n]).astype(BF16)

    def add_into(d, rows, parts):
        total = own[d, rows, :].astype(F32)
        for part in parts:
            total = total + part[rows, :].astype(F32)
        own[d, rows, :] = total.astype(BF16)

    mix = (
        (iota((256, 256), 0) >> 7 == iota((256, 256), 1) >> 7)
        & (
            iota((256, 256), 1) & 127
            == ((iota((256, 256), 0) & 127) >> 1) + 64 * (iota((256, 256), 0) & 1)
        )
    ).astype(F32).astype(BF16)

    hops = sorted(
        ((a, b) for a in range(4) for b in range(4) if a or b),
        key=lambda ab: -(min(ab[0], 4 - ab[0]) + min(ab[1], 4 - ab[1])),
    )
    targets = [(expert_at(a, b), place(zs[a], ys[b])) for a, b in hops]
    rest = pl.ds(CHUNK, ROWS - CHUNK)

    def relay(l, step, src, dst):
        return remote(src, dst, relay_s.at[l, step], relay_r.at[l, step], across)

    def dispatch_sent(l):
        relay(l, 0, xr, far_xr.at[l]).wait_send()
        remote(
            far_sl.at[rest, :], xf.at[l, 2, 0, rest, :], disp_s.at[l, 1], disp_r.at[l, 1, 0],
            sibling,
        ).wait_send()
        remote(
            sl.at[rest, :], xf.at[l, 0, 0, rest, :], disp_s.at[l, 0], disp_r.at[l, 0, 0],
            sibling,
        ).wait_send()

    def slot_values(l):
        gained = (stream[...] * gain_ref[pl.ds(l, 1), :]).astype(BF16)
        for h in range(2):
            xr[pl.ds(h * TOK, TOK), :] = dot(
                gained, had[:, h * HALF : (h + 1) * HALF]
            ).astype(BF16)

        @pl.loop(0, 4)
        def _(p):
            at = pl.ds(pl.multiple_of(p * GROUP, GROUP), GROUP)
            sl[at, :] = dot(gath[at, :], xr[...]).astype(BF16)

        return gained

    def to_experts(l, d, rows):
        which = 0 if d == 0 else 1
        for device, index in targets:
            remote(
                rows.at[chunk_at(index), :], xf.at[l, d, 0, chunk_at(mine), :],
                disp_s.at[l, which], disp_r.at[l, which, parity], device,
            ).start()
        pltpu.make_async_copy(
            rows.at[chunk_at(mine), :], xf.at[l, d, 0, chunk_at(mine), :],
            disp_r.at[l, which, parity],
        ).start()

    def relay_slots(l):
        relay(l, 0, xr, far_xr.at[l]).wait_recv()

        @pl.loop(0, 4)
        def _(p):
            at = pl.ds(pl.multiple_of(p * GROUP, GROUP), GROUP)
            far_sl[at, :] = dot(gath[at, :], far_xr[l]).astype(BF16)

        to_experts(l, 2, far_sl)

    def send_slots(l, gained):
        relay(l, 0, xr, far_xr.at[l]).start()
        to_experts(l, 0, sl)
        st = stream[...]
        squares = jnp.sum(st * st, axis=1, keepdims=True)
        logits = lax.dot_general(
            gained, rw_ref[l], (((1,), (1,)), ((), ())), preferred_element_type=F32
        )
        diff = jnp.sum(logits * sign, axis=1, keepdims=True)
        ex[l, 0] = jnp.where(iota((8, TOK), 0) == 0, as_row(squares), as_row(diff))
        for copy in exchange_copies(l):
            copy.start()

    def send_scales(l):
        all_of_exchange(l).wait_recv()
        total = ex[l, 0]
        for k in range(1, 8):
            total = total + ex[l, k]
        factor = lax.rsqrt(as_column(total[0:1, :]) / (8 * WIDTH) + 1e-05)
        weights[...] = 1.0 / (1.0 + jnp.exp(-factor * as_column(total[1:2, :])))
        at = iota((TOK, TOK), 1)
        for p in range(4):
            slot = (p * 4 + (at >> 5)) * CAP + (at & 31)
            hit = ((slot == slot_cols[0]) | (slot == slot_cols[1])) & ((at & 31) < CAP)
            row = jnp.sum(jnp.where(hit, factor, 0.0), axis=0, keepdims=True)
            scale_out[l, p] = jnp.broadcast_to(row, (8, TOK))
        for device, index in targets:
            remote(
                scale_out.at[l, lax.div(index, 4)], scales.at[l, mine], scale_s.at[l],
                scale_r.at[l, parity], device,
            ).start()
        pltpu.make_async_copy(
            scale_out.at[l, lax.div(mine, 4)], scales.at[l, mine], scale_r.at[l, parity]
        ).start()

    def combine(l):
        weight = weights[...]
        pltpu.make_async_copy(own.at[0], ret.at[l, 0], ret_r.at[l, 0]).wait()
        relay(l, 1, far_sum, far_in.at[l]).wait_recv()
        for h in range(2):
            part = pl.ds(h * TOK, TOK)
            first = dot(pick[0, part, :], ret[l, 0])
            second = dot(pick[1, part, :], ret[l, 0])
            columns = slice(h * HALF, (h + 1) * HALF)
            stream[:, columns] = (
                stream[:, columns] + weight * first + (1.0 - weight) * second
            ) + far_in[l, part, :].astype(F32)

    def relay_combine(l):
        weight = weights[...]
        pltpu.make_async_copy(own.at[2], ret.at[l, 1], ret_r.at[l, 1]).wait()
        for h in range(2):
            part = pl.ds(h * TOK, TOK)
            first = dot(pick[0, part, :], ret[l, 1])
            second = dot(pick[1, part, :], ret[l, 1])
            far_sum[part, :] = (weight * first + (1.0 - weight) * second).astype(BF16)
        relay(l, 1, far_sum, far_in.at[l]).start()

    def prepare(l):
        codes = code_copies(l)
        for copy in codes:
            copy.wait()

        @pl.loop(0, 16)
        def _(step):
            prepare_in(l, step)

        @pl.loop(0, 8)
        def _(n):
            prepare_out(l, n)

        @pl.when(l + 1 < LAYERS)
        def _():
            for copy in code_copies(l + 1):
                copy.start()

    def gather(l, s, kind, src, dst, device):
        rows = rows_of(2 * s, 2)
        return remote(
            xf.at[(l,) + src + (rows,)], xf.at[(l,) + dst + (rows,)],
            ag_s.at[l, kind], ag_r.at[l, kind, s], device,
        )

    def up_copy(l, s):
        return gather(l, s, 1, (0, 0), (3, 0), up)

    def down_copy(l, s):
        return gather(l, s, 2, (0, 0), (1, 0), down)

    def sib_copy(l, s, d):
        return gather(l, s, {0: 0, 3: 3, 1: 4, 2: 5}[d], (d, 0), (d, 1), sibling)

    def dispatched(l, s, d):
        arrived = xf.at[l, d, 0, rows_of(2 * s, 2), :]
        pltpu.make_async_copy(arrived, arrived, disp_r.at[l, d // 2, s]).wait()

    def send_own(l, s):
        dispatched(l, s, 0)
        up_copy(l, s).start()
        down_copy(l, s).start()
        sib_copy(l, s, 0).start()

    factor = 2.0**-10 / math.sqrt(8 * WIDTH)

    def hidden_own(l, s):
        multiply_in(l, s, 0, 0, first=True)
        sib_copy(l, s, 0).wait_recv()
        multiply_in(l, s, 0, 1)

    def hidden(l, s):
        dispatched(l, s, 2)
        sib_copy(l, s, 2).start()
        multiply_in(l, s, 2, 0)
        up_copy(l, s).wait_recv()
        sib_copy(l, s, 3).start()
        down_copy(l, s).wait_recv()
        sib_copy(l, s, 1).start()
        multiply_in(l, s, 3, 0)
        multiply_in(l, s, 1, 0)
        for d in (2, 3, 1):
            sib_copy(l, s, d).wait_recv()
            multiply_in(l, s, d, 1)

        eight = scales.at[l, pl.ds(8 * s, 8)]
        pltpu.make_async_copy(eight, eight, scale_r.at[l, s]).wait()
        lanes_of = iota((CAP, TOK), 1) == iota((CAP, TOK), 0) + lax.rem(mine, 4) * 32

        zero = jnp.zeros((CAP, 128), F32)

        @pl.loop(0, 8)
        def _(j):
            first = pl.ds(pl.multiple_of(j * CHUNK, 8), CAP)
            second = pl.ds(pl.multiple_of(j * CHUNK + CAP, 8), CAP)
            scale = jnp.sum(
                jnp.where(lanes_of, scales[l, 8 * s + j, 0:1, :], 0.0), axis=1, keepdims=True
            )
            total = (acc[first, 0:256] + acc[second, 256:512]) * (factor * scale)
            gate, value = total[:, 0:128], total[:, 128:256]
            act = gate / (1.0 + jnp.exp(-gate)) * value
            actx[first, 0:128] = act
            actx[first, 128:256] = zero
            actx[second, 0:128] = zero
            actx[second, 128:256] = act

        actp[rows_of(2 * s, 2), :] = dot(actx[...].astype(BF16), mix).astype(BF16)

    def sum_sib(l, s, d):
        rows = rows_of(2 * s, 2)
        return remote(
            pk1.at[d, rows, :], sibr.at[l, d, rows, :], rs_s.at[l, 0],
            rs_r.at[l, 0, 4 * s + d], sibling,
        )

    def sum_owner(l, s, d):
        kind = 1 if d == 1 else 2
        rows = rows_of(2 * s, 2)
        return remote(
            own.at[d, rows, :], rf.at[l, kind - 1, rows, :], rs_s.at[l, kind],
            rs_r.at[l, kind, s], up if d == 1 else down,
        )

    def to_sibling(l, s, d):
        multiply_out(s, d, 1)
        sum_sib(l, s, d).start()

    def chip_sum(l, s, d):
        sum_sib(l, s, d).wait_recv()
        for g in (2 * s, 2 * s + 1):
            add_into(d, rows_of(g), [sibr.at[l, d]])

    def to_homes(l, g, d):
        which = 0 if d == 0 else 1
        for q in range(4):
            to_z = 2 * (g % 2) + q // 2
            to_y = 2 * (q % 2) + (g // 2 + to_z) % 2
            src = own.at[d, pl.ds((g * 4 + q) * CHUNK, CHUNK), :]
            dst = ret.at[l, which, chunk_at(mine), :]
            here = e == to_z * 4 + to_y

            @pl.when(here)
            def _():
                pltpu.make_async_copy(src, dst, ret_r.at[l, which]).start()

            @pl.when(jnp.logical_not(here))
            def _():
                remote(
                    src, dst, ret_s.at[l, which], ret_r.at[l, which],
                    {"expert": to_z * 4 + to_y, "tensor": t},
                ).start()

    def sums(l, s):
        to_sibling(l, s, 1)
        multiply_out(s, 1, 0)
        to_sibling(l, s, 3)
        chip_sum(l, s, 1)
        sum_owner(l, s, 1).start()
        multiply_out(s, 3, 0)
        to_sibling(l, s, 2)
        chip_sum(l, s, 3)
        sum_owner(l, s, 3).start()
        multiply_out(s, 2, 0)
        to_sibling(l, s, 0)
        chip_sum(l, s, 2)
        to_homes(l, 2 * s, 2)
        to_homes(l, 2 * s + 1, 2)
        multiply_out(s, 0, 0)

    def give_back(l, s):
        sum_sib(l, s, 0).wait_recv()
        sum_owner(l, s, 1).wait_recv()
        sum_owner(l, s, 3).wait_recv()
        for g in (2 * s, 2 * s + 1):
            add_into(0, rows_of(g), [sibr.at[l, 0], rf.at[l, 0], rf.at[l, 1]])
            to_homes(l, g, 0)

    def all_sent(l):
        all_of_exchange(l).wait_send()
        fifteen = scales.at[l, pl.ds(0, 15)]
        remote(fifteen, fifteen, scale_s.at[l], scale_r.at[l, 0], sibling).wait_send()
        for kind in range(6):
            remote(
                xf.at[l, 0, 0], xf.at[l, 0, 1], ag_s.at[l, kind], ag_r.at[l, kind, 0], sibling
            ).wait_send()
        remote(pk1, sibr.at[l], rs_s.at[l, 0], rs_r.at[l, 0, 0], sibling).wait_send()
        for kind in range(1, 3):
            remote(
                own.at[1], rf.at[l, 0], rs_s.at[l, kind], rs_r.at[l, kind, 0], sibling
            ).wait_send()
        for which in range(2):
            remote(
                own.at[0, rest, :], ret.at[l, which, rest, :], ret_s.at[l, which],
                ret_r.at[l, which], sibling,
            ).wait_send()
        relay(l, 1, far_sum, far_in.at[l]).wait_send()

    def finish(l):
        combine(l)

        @pl.when(l + 1 < LAYERS)
        def _():
            dispatch_sent(l)
            send_slots(l + 1, slot_values(l + 1))

    def layer(l, carry):
        @pl.when((l > 0) & (parity == 0))
        def _():
            relay_slots(l)
            send_scales(l)

        send_own(l, 0)

        @pl.when((l > 0) & (parity == 1))
        def _():
            finish(l - 1)

        hidden_own(l, 0)

        @pl.when(l == 0)
        def _():
            relay_slots(0)
            send_scales(0)
            send_own(0, 1)

        @pl.when((l > 0) & (parity == 1))
        def _():
            relay_slots(l)
            send_scales(l)

        hidden(l, 0)

        @pl.when(l > 0)
        def _():
            all_sent(l - 1)
            send_own(l, 1)

        sums(l, 0)
        hidden_own(l, 1)
        hidden(l, 1)
        sums(l, 1)

        @pl.when(l + 1 < LAYERS)
        def _():
            prepare(l + 1)

        @pl.when(parity == 0)
        def _():
            relay_combine(l)

        give_back(l, 0)

        @pl.when(parity == 0)
        def _():
            finish(l)

        @pl.when(parity == 1)
        def _():
            relay_combine(l)

        give_back(l, 1)
        return carry

    gained = slot_values(0)
    pl.semaphore_wait(barrier, 22)

    @pl.when(parity == 1)
    def _():
        prepare(0)

    send_slots(0, gained)

    @pl.when(parity == 0)
    def _():
        prepare(0)

    lane = iota((1, ROWS), 1)
    lane_chunk = lane // CHUNK
    lane_inner = lane - lane_chunk * CHUNK
    lane_half = (lane_inner >= CAP).astype(I32)
    lane_slot = lane_chunk * CAP + lane_inner - lane_half * CAP
    for k in range(2):
        for h in range(2):
            hit = (lane_half == h) & (lane_slot == slot_cols[k])
            pick[k, pl.ds(h * TOK, TOK), :] = hit.astype(F32).astype(BF16)

    lax.fori_loop(0, LAYERS, layer, 0)

    @pl.when(parity == 1)
    def _():
        combine(LAYERS - 1)

    dispatch_sent(LAYERS - 1)
    all_sent(LAYERS - 1)
    out_ref[...] = stream[...].astype(BF16)


def per_device(
    tokens, routes, norm_gain, router_weight, gate_codes, gate_scales, up_codes, up_scales,
    down_codes, down_scales,
):
    vmem = pl.BlockSpec(memory_space=pltpu.VMEM)
    anywhere = pl.BlockSpec(memory_space=pl.ANY)
    dma = pltpu.SemaphoreType.DMA
    return pl.pallas_call(
        kernel,
        out_shape=jax.ShapeDtypeStruct((TOK, WIDTH), BF16),
        in_specs=[
            vmem, vmem, vmem, vmem, anywhere, vmem, anywhere, vmem, anywhere, vmem,
        ],
        out_specs=vmem,
        scratch_shapes=[
            pltpu.VMEM((TOK, WIDTH), F32),
            pltpu.VMEM((WIDTH, WIDTH), BF16),
            pltpu.VMEM((4096, 128), I32),
            pltpu.VMEM((4096, 128), I32),
            pltpu.VMEM((64, 8192), I32),
            pltpu.VMEM((8, HALF, HALF), BF16),
            pltpu.VMEM((8, 256, HALF), BF16),
            pltpu.VMEM((ROWS, 2 * TOK), BF16),
            pltpu.VMEM((2, 2 * TOK, ROWS), BF16),
            pltpu.VMEM((2 * TOK, HALF), BF16),
            pltpu.VMEM((ROWS, HALF), BF16),
            pltpu.VMEM((LAYERS, 4, 2, ROWS, HALF), BF16),
            pltpu.VMEM((PART, HALF), F32),
            pltpu.VMEM((PART, 256), F32),
            pltpu.VMEM((ROWS, 256), BF16),
            pltpu.VMEM((4, ROWS, HALF), BF16),
            pltpu.VMEM((4, ROWS, HALF), BF16),
            pltpu.VMEM((LAYERS, 4, ROWS, HALF), BF16),
            pltpu.VMEM((LAYERS, 2, ROWS, HALF), BF16),
            pltpu.VMEM((LAYERS, 2, ROWS, HALF), BF16),
            pltpu.VMEM((LAYERS, 2 * TOK, HALF), BF16),
            pltpu.VMEM((ROWS, HALF), BF16),
            pltpu.VMEM((2 * TOK, HALF), BF16),
            pltpu.VMEM((LAYERS, 2 * TOK, HALF), BF16),
            pltpu.VMEM((LAYERS, 8, 8, TOK), F32),
            pltpu.VMEM((TOK, 1), F32),
            pltpu.VMEM((LAYERS, 4, 8, TOK), F32),
            pltpu.VMEM((LAYERS, 16, 8, TOK), F32),
            dma((3,)),
            dma((LAYERS,)), dma((LAYERS,)),
            dma((LAYERS,)), dma((LAYERS, 2)),
            dma((LAYERS, 2)), dma((LAYERS, 2, 2)),
            dma((LAYERS, 6)), dma((LAYERS, 6, 2)),
            dma((LAYERS, 3)), dma((LAYERS, 3, 8)),
            dma((LAYERS, 2)), dma((LAYERS, 2)),
            dma((LAYERS, 2)), dma((LAYERS, 2)),
        ],
        compiler_params=pltpu.CompilerParams(
            collective_id=0, has_side_effects=True, vmem_limit_bytes=60 << 20
        ),
        name="moe_layers",
    )(
        tokens, routes.T, norm_gain, router_weight.transpose(0, 2, 1),
        gate_codes.reshape(LAYERS, 4096, 128),
        gate_scales.reshape(LAYERS, 64, 128), up_codes.reshape(LAYERS, 4096, 128),
        up_scales.reshape(LAYERS, 64, 128), down_codes.reshape(LAYERS, 64, 8192),
        down_scales.reshape(LAYERS, 1, 8192),
    )


def solution(mesh):
    in_specs = (
        P("expert", "tensor"),
        P("expert", None),
        P(None, "tensor"),
        P(None, "tensor", None),
        P(None, "expert", None, "tensor"),
        P(None, "expert", None, "tensor"),
        P(None, "expert", None, "tensor"),
        P(None, "expert", None, "tensor"),
        P(None, "expert", "tensor", None),
        P(None, "expert", "tensor", None),
    )
    return jax.shard_map(
        per_device, mesh=mesh, in_specs=in_specs, out_specs=P("expert", "tensor"),
        check_vma=False,
    )
```

```python
import functools
import math

import jax
import jax.numpy as jnp
from jax import lax
from jax.experimental import pallas as pl
from jax.experimental.pallas import tpu as pltpu
from jax.sharding import PartitionSpec as P

LAYERS = 2
TOK = 128
WIDTH = 1024
HALF = 512
CAP = 24
CHUNK = 2 * CAP
ROWS = 16 * CHUNK
GROUP = 4 * CHUNK
PART = 2 * GROUP
MESH = pl.DeviceIdType.MESH
F32 = jnp.float32
BF16 = jnp.bfloat16
I32 = jnp.int32


def dot(a, b):
    return jnp.dot(a, b, preferred_element_type=F32)


def place(z, y):
    return lax.rem(z + y, 2) * 8 + z * 2 + lax.div(y, 2)


def chunk_at(index):
    return pl.ds(pl.multiple_of(index * CHUNK, CHUNK), CHUNK)


def iota(shape, dim):
    return lax.broadcasted_iota(I32, shape, dim)


def walsh(values):
    values = list(values)
    for bit in (1, 2, 4):
        for i in range(8):
            if not i & bit:
                low, high = values[i], values[i | bit]
                values[i], values[i | bit] = low + high, low - high
    return values


def rows_of(group, count=1):
    return pl.ds(group * GROUP, count * GROUP)


def kernel(
    tok_ref, routes_ref, gain_ref, rw_ref, gc_hbm, gs_ref, uc_hbm, us_ref, dc_hbm, ds_ref,
    out_ref,
    stream, had, cg, cu, cd, wp, wd, gath, pick, xr, sl, xf, acc, actx, actp,
    own, pk1, sibr, rf, ret, far_xr, far_sl, far_sum, far_in, ex, weights, scale_out, scales,
    code_sem, ex_s, ex_r, scale_s, scale_r, disp_s, disp_r, ag_s, ag_r, rs_s, rs_r, ret_s, ret_r, relay_s, relay_r,
):
    e = lax.axis_index("expert")
    t = lax.axis_index("tensor")
    z, y = lax.div(e, 4), lax.rem(e, 4)
    x, c = lax.div(t, 2), lax.rem(t, 2)
    zs = [z] + [lax.rem(z + a, 4) for a in range(1, 4)]
    ys = [y] + [lax.rem(y + b, 4) for b in range(1, 4)]
    parity = lax.rem(z + y, 2)
    mine = place(z, y)
    xs = [x * 2] + [lax.rem(x + d, 4) * 2 for d in range(1, 4)]
    cores = [c, 1 - c]

    def expert_at(a, b):
        return {"expert": zs[a] * 4 + ys[b], "tensor": t}

    def tensor_at(index):
        return {"expert": e, "tensor": index}

    def block(d, k):
        return xs[d] + cores[k]

    sibling = tensor_at(block(0, 1))
    up = tensor_at(block(1, 0))
    down = tensor_at(block(3, 0))
    across = tensor_at(block(2, 0))
    others = [tensor_at(lax.rem(t + k, 8)) for k in range(1, 8)]

    def remote(src, dst, ssem, rsem, device):
        return pltpu.make_async_remote_copy(
            src_ref=src, dst_ref=dst, send_sem=ssem, recv_sem=rsem,
            device_id=device, device_id_type=MESH,
        )

    def code_copies(l):
        return [
            pltpu.make_async_copy(gc_hbm.at[l], cg, code_sem.at[0]),
            pltpu.make_async_copy(uc_hbm.at[l], cu, code_sem.at[1]),
            pltpu.make_async_copy(dc_hbm.at[l], cd, code_sem.at[2]),
        ]

    barrier = pltpu.get_barrier_semaphore()
    for a in range(4):
        for b in range(4):
            if a or b:
                pl.semaphore_signal(
                    barrier, inc=1, device_id=expert_at(a, b), device_id_type=MESH
                )
    for other in others:
        pl.semaphore_signal(barrier, inc=1, device_id=other, device_id_type=MESH)

    for copy in code_copies(0):
        copy.start()
    eye = (iota((TOK, TOK), 0) == iota((TOK, TOK), 1)).astype(F32)
    stream[...] = tok_ref[...].astype(F32)

    def exchange_copies(l):
        return [
            remote(ex.at[l, 0], ex.at[l, k], ex_s.at[l], ex_r.at[l], others[k - 1])
            for k in range(1, 8)
        ]

    def all_of_exchange(l):
        seven = ex.at[l, pl.ds(1, 7)]
        return remote(seven, seven, ex_s.at[l], ex_r.at[l], sibling)

    def as_row(column):
        return jnp.sum(eye * column, axis=0, keepdims=True)

    def as_column(row):
        return jnp.sum(eye * row, axis=1, keepdims=True)

    below = (iota((TOK, TOK), 0) > iota((TOK, TOK), 1)).astype(BF16)
    lanes = iota((TOK, 16), 1)
    picks, rels = [], []
    for k in range(2):
        named = jnp.sum(
            eye * routes_ref[k : k + 1, :].astype(F32), axis=1, keepdims=True
        ).astype(I32)
        picks.append((named == lanes).astype(F32))
        to_z, to_y = named >> 2, named & 3
        rels.append(((to_z + to_y) & 1) * 8 + to_z * 2 + (to_y >> 1))
    earlier = dot(below, (picks[0] + picks[1]).astype(BF16))
    slots = []
    for k in range(2):
        rank = jnp.sum(picks[k] * earlier, axis=1, keepdims=True)
        slots.append(rels[k].astype(F32) * CAP + rank)
    slot_rows = [as_row(s).astype(I32) for s in slots]
    slot_cols = [s.astype(I32) for s in slots]
    sign = picks[0] - picks[1]

    row = iota((ROWS, 1), 0)
    chunk = row // CHUNK
    inner = row - chunk * CHUNK
    row_half = (inner >= CAP).astype(I32)
    row_slot = chunk * CAP + inner - row_half * CAP
    col_half = (iota((1, 2 * TOK), 1) >= TOK).astype(I32)
    both = [jnp.concatenate([s, s], axis=1) for s in slot_rows]
    hit = (row_half == col_half) & ((row_slot == both[0]) | (row_slot == both[1]))
    gath[...] = hit.astype(F32).astype(BF16)

    @pl.loop(0, 32)
    def _(i):
        at = pl.multiple_of(i * 32, 32)
        r = iota((32, WIDTH), 0) + at
        j = iota((32, WIDTH), 1)
        v = r & (2 * (j & (HALF - 1)) + (j >> 9))
        v = v ^ (v >> 8)
        v = v ^ (v >> 4)
        v = v ^ (v >> 2)
        v = v ^ (v >> 1)
        had[pl.ds(at, 32), :] = (1 - 2 * (v & 1)).astype(F32).astype(BF16)

    def prepare_in(l, step):
        at = pl.multiple_of(step * 32, 32)
        for kind, (codes, scales) in enumerate(((cg, gs_ref), (cu, us_ref))):
            words = [codes[pl.ds(m * HALF + at, 32), :] for m in range(8)]
            shifts = [10 - scales[l, pl.ds(m * 8 + step // 2, 1), :] for m in range(8)]
            for k in range(2):
                values = walsh(
                    ((((w >> (4 * k)) & 15) - 8) << s) for w, s in zip(words, shifts)
                )
                column = k * 256 + kind * 128
                for n in range(8):
                    wp[n, pl.ds(at, 32), column : column + 128] = (
                        values[n].astype(F32).astype(BF16)
                    )

    def prepare_out(l, n):
        for h in range(2):
            at = pl.multiple_of(n * WIDTH + h * HALF, HALF)
            words = cd[:, pl.ds(at, HALF)]
            shift = 8 - ds_ref[l, :, pl.ds(at, HALF)]
            for k in range(2):
                value = (((words >> (4 * k)) & 15) - 8) << shift
                wd[n, pl.ds(h * 128 + k * 64, 64), :] = (
                    value.astype(F32) * (2.0**-8)
                ).astype(BF16)

    def multiply_in(l, s, d, k, first=False):
        n = block(d, k)

        @pl.loop(0, 2)
        def _(i):
            at = pl.ds(pl.multiple_of(i * GROUP, GROUP), GROUP)
            rows = pl.ds(pl.multiple_of((2 * s + i) * GROUP, GROUP), GROUP)
            value = dot(xf[l, d, k, rows, :], wp[n])
            if first:
                acc[at, :] = value
            else:
                acc[at, :] += value

    def multiply_out(s, d, k):
        n = block(d, k)
        target = own if k == 0 else pk1

        @pl.loop(2 * s, 2 * s + 2)
        def _(g):
            at = pl.ds(pl.multiple_of(g * GROUP, GROUP), GROUP)
            target[d, at, :] = dot(actp[at, :], wd[n]).astype(BF16)

    def add_into(d, rows, parts):
        total = own[d, rows, :].astype(F32)
        for part in parts:
            total = total + part[rows, :].astype(F32)
        own[d, rows, :] = total.astype(BF16)

    mix = (
        (iota((256, 256), 0) >> 7 == iota((256, 256), 1) >> 7)
        & (
            iota((256, 256), 1) & 127
            == ((iota((256, 256), 0) & 127) >> 1) + 64 * (iota((256, 256), 0) & 1)
        )
    ).astype(F32).astype(BF16)

    hops = sorted(
        ((a, b) for a in range(4) for b in range(4) if a or b),
        key=lambda ab: -(min(ab[0], 4 - ab[0]) + min(ab[1], 4 - ab[1])),
    )
    targets = [(expert_at(a, b), place(zs[a], ys[b])) for a, b in hops]
    rest = pl.ds(CHUNK, ROWS - CHUNK)

    def relay(l, step, src, dst):
        return remote(src, dst, relay_s.at[l, step], relay_r.at[l, step], across)

    def dispatch_sent(l):
        relay(l, 0, xr, far_xr.at[l]).wait_send()
        remote(
            far_sl.at[rest, :], xf.at[l, 2, 0, rest, :], disp_s.at[l, 1], disp_r.at[l, 1, 0],
            sibling,
        ).wait_send()
        remote(
            sl.at[rest, :], xf.at[l, 0, 0, rest, :], disp_s.at[l, 0], disp_r.at[l, 0, 0],
            sibling,
        ).wait_send()

    def slot_values(l):
        gained = (stream[...] * gain_ref[pl.ds(l, 1), :]).astype(BF16)
        for h in range(2):
            xr[pl.ds(h * TOK, TOK), :] = dot(
                gained, had[:, h * HALF : (h + 1) * HALF]
            ).astype(BF16)

        @pl.loop(0, 4)
        def _(p):
            at = pl.ds(pl.multiple_of(p * GROUP, GROUP), GROUP)
            sl[at, :] = dot(gath[at, :], xr[...]).astype(BF16)

        return gained

    def to_experts(l, d, rows):
        which = 0 if d == 0 else 1
        for device, index in targets:
            remote(
                rows.at[chunk_at(index), :], xf.at[l, d, 0, chunk_at(mine), :],
                disp_s.at[l, which], disp_r.at[l, which, parity], device,
            ).start()
        pltpu.make_async_copy(
            rows.at[chunk_at(mine), :], xf.at[l, d, 0, chunk_at(mine), :],
            disp_r.at[l, which, parity],
        ).start()

    def relay_slots(l):
        relay(l, 0, xr, far_xr.at[l]).wait_recv()

        @pl.loop(0, 4)
        def _(p):
            at = pl.ds(pl.multiple_of(p * GROUP, GROUP), GROUP)
            far_sl[at, :] = dot(gath[at, :], far_xr[l]).astype(BF16)

        to_experts(l, 2, far_sl)

    def send_slots(l, gained):
        relay(l, 0, xr, far_xr.at[l]).start()
        to_experts(l, 0, sl)
        st = stream[...]
        squares = jnp.sum(st * st, axis=1, keepdims=True)
        logits = lax.dot_general(
            gained, rw_ref[l], (((1,), (1,)), ((), ())), preferred_element_type=F32
        )
        diff = jnp.sum(logits * sign, axis=1, keepdims=True)
        ex[l, 0] = jnp.where(iota((8, TOK), 0) == 0, as_row(squares), as_row(diff))
        for copy in exchange_copies(l):
            copy.start()

    def send_scales(l):
        all_of_exchange(l).wait_recv()
        total = ex[l, 0]
        for k in range(1, 8):
            total = total + ex[l, k]
        factor = lax.rsqrt(as_column(total[0:1, :]) / (8 * WIDTH) + 1e-05)
        weights[...] = 1.0 / (1.0 + jnp.exp(-factor * as_column(total[1:2, :])))
        at = iota((TOK, TOK), 1)
        for p in range(4):
            slot = (p * 4 + (at >> 5)) * CAP + (at & 31)
            hit = ((slot == slot_cols[0]) | (slot == slot_cols[1])) & ((at & 31) < CAP)
            row = jnp.sum(jnp.where(hit, factor, 0.0), axis=0, keepdims=True)
            scale_out[l, p] = jnp.broadcast_to(row, (8, TOK))
        for device, index in targets:
            remote(
                scale_out.at[l, lax.div(index, 4)], scales.at[l, mine], scale_s.at[l],
                scale_r.at[l, parity], device,
            ).start()
        pltpu.make_async_copy(
            scale_out.at[l, lax.div(mine, 4)], scales.at[l, mine], scale_r.at[l, parity]
        ).start()

    def combine(l):
        weight = weights[...]
        pltpu.make_async_copy(own.at[0], ret.at[l, 0], ret_r.at[l, 0]).wait()
        relay(l, 1, far_sum, far_in.at[l]).wait_recv()
        for h in range(2):
            part = pl.ds(h * TOK, TOK)
            first = dot(pick[0, part, :], ret[l, 0])
            second = dot(pick[1, part, :], ret[l, 0])
            columns = slice(h * HALF, (h + 1) * HALF)
            stream[:, columns] = (
                stream[:, columns] + weight * first + (1.0 - weight) * second
            ) + far_in[l, part, :].astype(F32)

    def relay_combine(l):
        weight = weights[...]
        pltpu.make_async_copy(own.at[2], ret.at[l, 1], ret_r.at[l, 1]).wait()
        for h in range(2):
            part = pl.ds(h * TOK, TOK)
            first = dot(pick[0, part, :], ret[l, 1])
            second = dot(pick[1, part, :], ret[l, 1])
            far_sum[part, :] = (weight * first + (1.0 - weight) * second).astype(BF16)
        relay(l, 1, far_sum, far_in.at[l]).start()

    def prepare(l):
        codes = code_copies(l)
        for copy in codes:
            copy.wait()

        @pl.loop(0, 16)
        def _(step):
            prepare_in(l, step)

        @pl.loop(0, 8)
        def _(n):
            prepare_out(l, n)

        @pl.when(l + 1 < LAYERS)
        def _():
            for copy in code_copies(l + 1):
                copy.start()

    def gather(l, s, kind, src, dst, device):
        rows = rows_of(2 * s, 2)
        return remote(
            xf.at[(l,) + src + (rows,)], xf.at[(l,) + dst + (rows,)],
            ag_s.at[l, kind], ag_r.at[l, kind, s], device,
        )

    def up_copy(l, s):
        return gather(l, s, 1, (0, 0), (3, 0), up)

    def down_copy(l, s):
        return gather(l, s, 2, (0, 0), (1, 0), down)

    def sib_copy(l, s, d):
        return gather(l, s, {0: 0, 3: 3, 1: 4, 2: 5}[d], (d, 0), (d, 1), sibling)

    def dispatched(l, s, d):
        arrived = xf.at[l, d, 0, rows_of(2 * s, 2), :]
        pltpu.make_async_copy(arrived, arrived, disp_r.at[l, d // 2, s]).wait()

    def send_own(l, s):
        dispatched(l, s, 0)
        up_copy(l, s).start()
        down_copy(l, s).start()
        sib_copy(l, s, 0).start()

    factor = 2.0**-10 / math.sqrt(8 * WIDTH)

    def hidden_own(l, s):
        multiply_in(l, s, 0, 0, first=True)
        sib_copy(l, s, 0).wait_recv()
        multiply_in(l, s, 0, 1)

    def hidden(l, s):
        up_copy(l, s).wait_recv()
        sib_copy(l, s, 3).start()
        down_copy(l, s).wait_recv()
        sib_copy(l, s, 1).start()
        multiply_in(l, s, 3, 0)
        multiply_in(l, s, 1, 0)
        dispatched(l, s, 2)
        sib_copy(l, s, 2).start()
        multiply_in(l, s, 2, 0)
        for d in (3, 1, 2):
            sib_copy(l, s, d).wait_recv()
            multiply_in(l, s, d, 1)

        eight = scales.at[l, pl.ds(8 * s, 8)]
        pltpu.make_async_copy(eight, eight, scale_r.at[l, s]).wait()
        lanes_of = iota((CAP, TOK), 1) == iota((CAP, TOK), 0) + lax.rem(mine, 4) * 32

        zero = jnp.zeros((CAP, 128), F32)

        @pl.loop(0, 8)
        def _(j):
            first = pl.ds(pl.multiple_of(j * CHUNK, 8), CAP)
            second = pl.ds(pl.multiple_of(j * CHUNK + CAP, 8), CAP)
            scale = jnp.sum(
                jnp.where(lanes_of, scales[l, 8 * s + j, 0:1, :], 0.0), axis=1, keepdims=True
            )
            total = (acc[first, 0:256] + acc[second, 256:512]) * (factor * scale)
            gate, value = total[:, 0:128], total[:, 128:256]
            act = gate / (1.0 + jnp.exp(-gate)) * value
            actx[first, 0:128] = act
            actx[first, 128:256] = zero
            actx[second, 0:128] = zero
            actx[second, 128:256] = act

        actp[rows_of(2 * s, 2), :] = dot(actx[...].astype(BF16), mix).astype(BF16)

    def sum_sib(l, s, d):
        rows = rows_of(2 * s, 2)
        return remote(
            pk1.at[d, rows, :], sibr.at[l, d, rows, :], rs_s.at[l, 0],
            rs_r.at[l, 0, 4 * s + d], sibling,
        )

    def sum_owner(l, s, d):
        kind = 1 if d == 1 else 2
        rows = rows_of(2 * s, 2)
        return remote(
            own.at[d, rows, :], rf.at[l, kind - 1, rows, :], rs_s.at[l, kind],
            rs_r.at[l, kind, s], up if d == 1 else down,
        )

    def to_sibling(l, s, d):
        multiply_out(s, d, 1)
        sum_sib(l, s, d).start()

    def chip_sum(l, s, d):
        sum_sib(l, s, d).wait_recv()
        for g in (2 * s, 2 * s + 1):
            add_into(d, rows_of(g), [sibr.at[l, d]])

    def to_homes(l, s, d):
        which = 0 if d == 0 else 1
        for i in range(8):
            low = lax.rem(mine + i, 8)
            to_z = lax.div(low, 2)
            to_y = 2 * lax.rem(low, 2) + lax.rem(to_z + s, 2)
            src = own.at[d, chunk_at(low + 8 * s), :]
            dst = ret.at[l, which, chunk_at(mine), :]
            away = remote(
                src, dst, ret_s.at[l, which], ret_r.at[l, which],
                {"expert": to_z * 4 + to_y, "tensor": t},
            )
            if i:
                away.start()
                continue

            @pl.when(parity == s)
            def _():
                pltpu.make_async_copy(src, dst, ret_r.at[l, which]).start()

            @pl.when(parity != s)
            def _():
                away.start()

    def sums(l, s):
        to_sibling(l, s, 1)
        multiply_out(s, 1, 0)
        to_sibling(l, s, 3)
        chip_sum(l, s, 1)
        sum_owner(l, s, 1).start()
        multiply_out(s, 3, 0)
        to_sibling(l, s, 2)
        chip_sum(l, s, 3)
        sum_owner(l, s, 3).start()
        multiply_out(s, 2, 0)
        to_sibling(l, s, 0)
        chip_sum(l, s, 2)
        to_homes(l, s, 2)
        multiply_out(s, 0, 0)

    def give_back(l, s):
        sum_sib(l, s, 0).wait_recv()
        sum_owner(l, s, 1).wait_recv()
        sum_owner(l, s, 3).wait_recv()
        for g in (2 * s, 2 * s + 1):
            add_into(0, rows_of(g), [sibr.at[l, 0], rf.at[l, 0], rf.at[l, 1]])
        to_homes(l, s, 0)

    def all_sent(l):
        all_of_exchange(l).wait_send()
        fifteen = scales.at[l, pl.ds(0, 15)]
        remote(fifteen, fifteen, scale_s.at[l], scale_r.at[l, 0], sibling).wait_send()
        for kind in range(6):
            remote(
                xf.at[l, 0, 0], xf.at[l, 0, 1], ag_s.at[l, kind], ag_r.at[l, kind, 0], sibling
            ).wait_send()
        remote(pk1, sibr.at[l], rs_s.at[l, 0], rs_r.at[l, 0, 0], sibling).wait_send()
        for kind in range(1, 3):
            remote(
                own.at[1], rf.at[l, 0], rs_s.at[l, kind], rs_r.at[l, kind, 0], sibling
            ).wait_send()
        for which in range(2):
            remote(
                own.at[0, rest, :], ret.at[l, which, rest, :], ret_s.at[l, which],
                ret_r.at[l, which], sibling,
            ).wait_send()
        relay(l, 1, far_sum, far_in.at[l]).wait_send()

    def finish(l):
        combine(l)

        @pl.when(l + 1 < LAYERS)
        def _():
            dispatch_sent(l)
            send_slots(l + 1, slot_values(l + 1))

    def layer(l, carry):
        @pl.when((l > 0) & (parity == 0))
        def _():
            relay_slots(l)
            send_scales(l)

        @pl.when((l > 0) & (parity == 1))
        def _():
            finish(l - 1)

        send_own(l, 0)
        hidden_own(l, 0)

        @pl.when(l == 0)
        def _():
            relay_slots(0)
            send_scales(0)
            send_own(0, 1)

        @pl.when((l > 0) & (parity == 1))
        def _():
            relay_slots(l)
            send_scales(l)

        @pl.when(l > 0)
        def _():
            send_own(l, 1)

        hidden(l, 0)

        @pl.when(l > 0)
        def _():
            all_sent(l - 1)

        sums(l, 0)
        hidden_own(l, 1)
        hidden(l, 1)
        sums(l, 1)

        @pl.when(l + 1 < LAYERS)
        def _():
            prepare(l + 1)

        @pl.when(parity == 0)
        def _():
            relay_combine(l)

        give_back(l, 0)

        @pl.when(parity == 1)
        def _():
            relay_combine(l)

        give_back(l, 1)

        @pl.when(parity == 0)
        def _():
            finish(l)

        return carry

    gained = slot_values(0)
    pl.semaphore_wait(barrier, 22)

    @pl.when(parity == 1)
    def _():
        prepare(0)

    send_slots(0, gained)

    @pl.when(parity == 0)
    def _():
        prepare(0)

    lane = iota((1, ROWS), 1)
    lane_chunk = lane // CHUNK
    lane_inner = lane - lane_chunk * CHUNK
    lane_half = (lane_inner >= CAP).astype(I32)
    lane_slot = lane_chunk * CAP + lane_inner - lane_half * CAP
    for k in range(2):
        for h in range(2):
            hit = (lane_half == h) & (lane_slot == slot_cols[k])
            pick[k, pl.ds(h * TOK, TOK), :] = hit.astype(F32).astype(BF16)

    lax.fori_loop(0, LAYERS, layer, 0)

    @pl.when(parity == 1)
    def _():
        combine(LAYERS - 1)

    dispatch_sent(LAYERS - 1)
    all_sent(LAYERS - 1)
    out_ref[...] = stream[...].astype(BF16)


def per_device(
    tokens, routes, norm_gain, router_weight, gate_codes, gate_scales, up_codes, up_scales,
    down_codes, down_scales,
):
    vmem = pl.BlockSpec(memory_space=pltpu.VMEM)
    anywhere = pl.BlockSpec(memory_space=pl.ANY)
    dma = pltpu.SemaphoreType.DMA
    return pl.pallas_call(
        kernel,
        out_shape=jax.ShapeDtypeStruct((TOK, WIDTH), BF16),
        in_specs=[
            vmem, vmem, vmem, vmem, anywhere, vmem, anywhere, vmem, anywhere, vmem,
        ],
        out_specs=vmem,
        scratch_shapes=[
            pltpu.VMEM((TOK, WIDTH), F32),
            pltpu.VMEM((WIDTH, WIDTH), BF16),
            pltpu.VMEM((4096, 128), I32),
            pltpu.VMEM((4096, 128), I32),
            pltpu.VMEM((64, 8192), I32),
            pltpu.VMEM((8, HALF, HALF), BF16),
            pltpu.VMEM((8, 256, HALF), BF16),
            pltpu.VMEM((ROWS, 2 * TOK), BF16),
            pltpu.VMEM((2, 2 * TOK, ROWS), BF16),
            pltpu.VMEM((2 * TOK, HALF), BF16),
            pltpu.VMEM((ROWS, HALF), BF16),
            pltpu.VMEM((LAYERS, 4, 2, ROWS, HALF), BF16),
            pltpu.VMEM((PART, HALF), F32),
            pltpu.VMEM((PART, 256), F32),
            pltpu.VMEM((ROWS, 256), BF16),
            pltpu.VMEM((4, ROWS, HALF), BF16),
            pltpu.VMEM((4, ROWS, HALF), BF16),
            pltpu.VMEM((LAYERS, 4, ROWS, HALF), BF16),
            pltpu.VMEM((LAYERS, 2, ROWS, HALF), BF16),
            pltpu.VMEM((LAYERS, 2, ROWS, HALF), BF16),
            pltpu.VMEM((LAYERS, 2 * TOK, HALF), BF16),
            pltpu.VMEM((ROWS, HALF), BF16),
            pltpu.VMEM((2 * TOK, HALF), BF16),
            pltpu.VMEM((LAYERS, 2 * TOK, HALF), BF16),
            pltpu.VMEM((LAYERS, 8, 8, TOK), F32),
            pltpu.VMEM((TOK, 1), F32),
            pltpu.VMEM((LAYERS, 4, 8, TOK), F32),
            pltpu.VMEM((LAYERS, 16, 8, TOK), F32),
            dma((3,)),
            dma((LAYERS,)), dma((LAYERS,)),
            dma((LAYERS,)), dma((LAYERS, 2)),
            dma((LAYERS, 2)), dma((LAYERS, 2, 2)),
            dma((LAYERS, 6)), dma((LAYERS, 6, 2)),
            dma((LAYERS, 3)), dma((LAYERS, 3, 8)),
            dma((LAYERS, 2)), dma((LAYERS, 2)),
            dma((LAYERS, 2)), dma((LAYERS, 2)),
        ],
        compiler_params=pltpu.CompilerParams(
            collective_id=0, has_side_effects=True, vmem_limit_bytes=60 << 20
        ),
        name="moe_layers",
    )(
        tokens, routes.T, norm_gain, router_weight.transpose(0, 2, 1),
        gate_codes.reshape(LAYERS, 4096, 128),
        gate_scales.reshape(LAYERS, 64, 128), up_codes.reshape(LAYERS, 4096, 128),
        up_scales.reshape(LAYERS, 64, 128), down_codes.reshape(LAYERS, 64, 8192),
        down_scales.reshape(LAYERS, 1, 8192),
    )


def solution(mesh):
    in_specs = (
        P("expert", "tensor"),
        P("expert", None),
        P(None, "tensor"),
        P(None, "tensor", None),
        P(None, "expert", None, "tensor"),
        P(None, "expert", None, "tensor"),
        P(None, "expert", None, "tensor"),
        P(None, "expert", None, "tensor"),
        P(None, "expert", "tensor", None),
        P(None, "expert", "tensor", None),
    )
    return jax.shard_map(
        per_device, mesh=mesh, in_specs=in_specs, out_specs=P("expert", "tensor"),
        check_vma=False,
    )
```

```python
import functools
import math

import jax
import jax.numpy as jnp
from jax import lax
from jax.experimental import pallas as pl
from jax.experimental.pallas import tpu as pltpu
from jax.sharding import PartitionSpec as P

LAYERS = 2
TOK = 128
WIDTH = 1024
HALF = 512
CAP = 24
CHUNK = 2 * CAP
ROWS = 16 * CHUNK
GROUP = 4 * CHUNK
PART = 2 * GROUP
MESH = pl.DeviceIdType.MESH
F32 = jnp.float32
BF16 = jnp.bfloat16
I32 = jnp.int32


def dot(a, b):
    return jnp.dot(a, b, preferred_element_type=F32)


def place(z, y):
    return lax.rem(z + y, 2) * 8 + z * 2 + lax.div(y, 2)


def chunk_at(index):
    return pl.ds(pl.multiple_of(index * CHUNK, CHUNK), CHUNK)


def iota(shape, dim):
    return lax.broadcasted_iota(I32, shape, dim)


def walsh(values):
    values = list(values)
    for bit in (1, 2, 4):
        for i in range(8):
            if not i & bit:
                low, high = values[i], values[i | bit]
                values[i], values[i | bit] = low + high, low - high
    return values


def rows_of(group, count=1):
    return pl.ds(group * GROUP, count * GROUP)


def kernel(
    tok_ref, routes_ref, gain_ref, rw_ref, gc_hbm, gs_ref, uc_hbm, us_ref, dc_hbm, ds_ref,
    out_ref,
    stream, had, cg, cu, cd, wp, wd, gath, pick, xr, sl, xf, acc, actx, actp,
    own, pk1, sibr, rf, ret, far_xr, far_sl, far_sum, far_in, ex, weights, scale_out, scales,
    code_sem, ex_s, ex_r, scale_s, scale_r, disp_s, disp_r, ag_s, ag_r, rs_s, rs_r, ret_s, ret_r, relay_s, relay_r,
):
    e = lax.axis_index("expert")
    t = lax.axis_index("tensor")
    z, y = lax.div(e, 4), lax.rem(e, 4)
    x, c = lax.div(t, 2), lax.rem(t, 2)
    zs = [z] + [lax.rem(z + a, 4) for a in range(1, 4)]
    ys = [y] + [lax.rem(y + b, 4) for b in range(1, 4)]
    parity = lax.rem(z + y, 2)
    mine = place(z, y)
    xs = [x * 2] + [lax.rem(x + d, 4) * 2 for d in range(1, 4)]
    cores = [c, 1 - c]

    def expert_at(a, b):
        return {"expert": zs[a] * 4 + ys[b], "tensor": t}

    def tensor_at(index):
        return {"expert": e, "tensor": index}

    def block(d, k):
        return xs[d] + cores[k]

    sibling = tensor_at(block(0, 1))
    up = tensor_at(block(1, 0))
    down = tensor_at(block(3, 0))
    across = tensor_at(block(2, 0))
    others = [tensor_at(lax.rem(t + k, 8)) for k in range(1, 8)]

    def remote(src, dst, ssem, rsem, device):
        return pltpu.make_async_remote_copy(
            src_ref=src, dst_ref=dst, send_sem=ssem, recv_sem=rsem,
            device_id=device, device_id_type=MESH,
        )

    def code_copies(l):
        return [
            pltpu.make_async_copy(gc_hbm.at[l], cg, code_sem.at[0]),
            pltpu.make_async_copy(uc_hbm.at[l], cu, code_sem.at[1]),
            pltpu.make_async_copy(dc_hbm.at[l], cd, code_sem.at[2]),
        ]

    barrier = pltpu.get_barrier_semaphore()
    for a in range(4):
        for b in range(4):
            if a or b:
                pl.semaphore_signal(
                    barrier, inc=1, device_id=expert_at(a, b), device_id_type=MESH
                )
    for other in others:
        pl.semaphore_signal(barrier, inc=1, device_id=other, device_id_type=MESH)

    for copy in code_copies(0):
        copy.start()
    eye = (iota((TOK, TOK), 0) == iota((TOK, TOK), 1)).astype(F32)
    stream[...] = tok_ref[...].astype(F32)

    def exchange_copies(l):
        return [
            remote(ex.at[l, 0], ex.at[l, k], ex_s.at[l], ex_r.at[l], others[k - 1])
            for k in range(1, 8)
        ]

    def all_of_exchange(l):
        seven = ex.at[l, pl.ds(1, 7)]
        return remote(seven, seven, ex_s.at[l], ex_r.at[l], sibling)

    def as_row(column):
        return jnp.sum(eye * column, axis=0, keepdims=True)

    def as_column(row):
        return jnp.sum(eye * row, axis=1, keepdims=True)

    below = (iota((TOK, TOK), 0) > iota((TOK, TOK), 1)).astype(BF16)
    lanes = iota((TOK, 16), 1)
    picks, rels = [], []
    for k in range(2):
        named = jnp.sum(
            eye * routes_ref[k : k + 1, :].astype(F32), axis=1, keepdims=True
        ).astype(I32)
        picks.append((named == lanes).astype(F32))
        to_z, to_y = named >> 2, named & 3
        rels.append(((to_z + to_y) & 1) * 8 + to_z * 2 + (to_y >> 1))
    earlier = dot(below, (picks[0] + picks[1]).astype(BF16))
    slots = []
    for k in range(2):
        rank = jnp.sum(picks[k] * earlier, axis=1, keepdims=True)
        slots.append(rels[k].astype(F32) * CAP + rank)
    slot_rows = [as_row(s).astype(I32) for s in slots]
    slot_cols = [s.astype(I32) for s in slots]
    sign = picks[0] - picks[1]

    row = iota((ROWS, 1), 0)
    chunk = row // CHUNK
    inner = row - chunk * CHUNK
    row_half = (inner >= CAP).astype(I32)
    row_slot = chunk * CAP + inner - row_half * CAP
    col_half = (iota((1, 2 * TOK), 1) >= TOK).astype(I32)
    both = [jnp.concatenate([s, s], axis=1) for s in slot_rows]
    hit = (row_half == col_half) & ((row_slot == both[0]) | (row_slot == both[1]))
    gath[...] = hit.astype(F32).astype(BF16)

    @pl.loop(0, 32)
    def _(i):
        at = pl.multiple_of(i * 32, 32)
        r = iota((32, WIDTH), 0) + at
        j = iota((32, WIDTH), 1)
        v = r & (2 * (j & (HALF - 1)) + (j >> 9))
        v = v ^ (v >> 8)
        v = v ^ (v >> 4)
        v = v ^ (v >> 2)
        v = v ^ (v >> 1)
        had[pl.ds(at, 32), :] = (1 - 2 * (v & 1)).astype(F32).astype(BF16)

    def prepare_in(l, step):
        at = pl.multiple_of(step * 32, 32)
        for kind, (codes, scales) in enumerate(((cg, gs_ref), (cu, us_ref))):
            words = [codes[pl.ds(m * HALF + at, 32), :] for m in range(8)]
            shifts = [10 - scales[l, pl.ds(m * 8 + step // 2, 1), :] for m in range(8)]
            for k in range(2):
                values = walsh(
                    ((((w >> (4 * k)) & 15) - 8) << s) for w, s in zip(words, shifts)
                )
                column = k * 256 + kind * 128
                for n in range(8):
                    wp[n, pl.ds(at, 32), column : column + 128] = (
                        values[n].astype(F32).astype(BF16)
                    )

    def prepare_out(l, n):
        for h in range(2):
            at = pl.multiple_of(n * WIDTH + h * HALF, HALF)
            words = cd[:, pl.ds(at, HALF)]
            shift = 8 - ds_ref[l, :, pl.ds(at, HALF)]
            for k in range(2):
                value = (((words >> (4 * k)) & 15) - 8) << shift
                wd[n, pl.ds(h * 128 + k * 64, 64), :] = (
                    value.astype(F32) * (2.0**-8)
                ).astype(BF16)

    def multiply_in(l, s, d, k, first=False):
        value = dot(xf[l, d, k, rows_of(2 * s, 2), :], wp[block(d, k)])
        if first:
            acc[...] = value
        else:
            acc[...] += value

    def multiply_out(s, d, k):
        target = own if k == 0 else pk1
        rows = rows_of(2 * s, 2)
        target[d, rows, :] = dot(actp[rows, :], wd[block(d, k)]).astype(BF16)

    def add_into(d, rows, parts):
        total = own[d, rows, :].astype(F32)
        for part in parts:
            total = total + part[rows, :].astype(F32)
        own[d, rows, :] = total.astype(BF16)

    mix = (
        (iota((256, 256), 0) >> 7 == iota((256, 256), 1) >> 7)
        & (
            iota((256, 256), 1) & 127
            == ((iota((256, 256), 0) & 127) >> 1) + 64 * (iota((256, 256), 0) & 1)
        )
    ).astype(F32).astype(BF16)

    hops = sorted(
        ((a, b) for a in range(4) for b in range(4) if a or b),
        key=lambda ab: -(min(ab[0], 4 - ab[0]) + min(ab[1], 4 - ab[1])),
    )
    targets = [(expert_at(a, b), place(zs[a], ys[b])) for a, b in hops]
    rest = pl.ds(CHUNK, ROWS - CHUNK)

    def relay(l, step, src, dst):
        return remote(src, dst, relay_s.at[l, step], relay_r.at[l, step], across)

    def dispatch_sent(l):
        relay(l, 0, xr, far_xr.at[l]).wait_send()
        remote(
            far_sl.at[rest, :], xf.at[l, 2, 0, rest, :], disp_s.at[l, 1], disp_r.at[l, 1, 0],
            sibling,
        ).wait_send()
        remote(
            sl.at[rest, :], xf.at[l, 0, 0, rest, :], disp_s.at[l, 0], disp_r.at[l, 0, 0],
            sibling,
        ).wait_send()

    def slot_values(l, ready):
        gained = (stream[...] * gain_ref[pl.ds(l, 1), :]).astype(BF16)
        for h in range(2):
            xr[pl.ds(h * TOK, TOK), :] = dot(
                gained, had[:, h * HALF : (h + 1) * HALF]
            ).astype(BF16)

        if ready:
            relay(l, 0, xr, far_xr.at[l]).start()
        sl[...] = dot(gath[...], xr[...]).astype(BF16)
        return gained

    def to_experts(l, d, rows):
        which = 0 if d == 0 else 1
        for device, index in targets:
            remote(
                rows.at[chunk_at(index), :], xf.at[l, d, 0, chunk_at(mine), :],
                disp_s.at[l, which], disp_r.at[l, which, parity], device,
            ).start()
        pltpu.make_async_copy(
            rows.at[chunk_at(mine), :], xf.at[l, d, 0, chunk_at(mine), :],
            disp_r.at[l, which, parity],
        ).start()

    def relay_slots(l):
        relay(l, 0, xr, far_xr.at[l]).wait_recv()
        far_sl[...] = dot(gath[...], far_xr[l]).astype(BF16)
        to_experts(l, 2, far_sl)

    def send_slots(l, gained):
        to_experts(l, 0, sl)
        st = stream[...]
        squares = jnp.sum(st * st, axis=1, keepdims=True)
        logits = lax.dot_general(
            gained, rw_ref[l], (((1,), (1,)), ((), ())), preferred_element_type=F32
        )
        diff = jnp.sum(logits * sign, axis=1, keepdims=True)
        ex[l, 0] = jnp.where(iota((8, TOK), 0) == 0, as_row(squares), as_row(diff))
        for copy in exchange_copies(l):
            copy.start()

    def send_scales(l):
        all_of_exchange(l).wait_recv()
        total = ex[l, 0]
        for k in range(1, 8):
            total = total + ex[l, k]
        factor = lax.rsqrt(as_column(total[0:1, :]) / (8 * WIDTH) + 1e-05)
        weights[...] = 1.0 / (1.0 + jnp.exp(-factor * as_column(total[1:2, :])))
        at = iota((TOK, TOK), 1)
        for p in range(4):
            slot = (p * 4 + (at >> 5)) * CAP + (at & 31)
            hit = ((slot == slot_cols[0]) | (slot == slot_cols[1])) & ((at & 31) < CAP)
            row = jnp.sum(jnp.where(hit, factor, 0.0), axis=0, keepdims=True)
            scale_out[l, p] = jnp.broadcast_to(row, (8, TOK))
        for device, index in targets:
            remote(
                scale_out.at[l, lax.div(index, 4)], scales.at[l, mine], scale_s.at[l],
                scale_r.at[l, parity], device,
            ).start()
        pltpu.make_async_copy(
            scale_out.at[l, lax.div(mine, 4)], scales.at[l, mine], scale_r.at[l, parity]
        ).start()

    def combine(l):
        weight = weights[...]
        pltpu.make_async_copy(own.at[0], ret.at[l, 0], ret_r.at[l, 0]).wait()
        relay(l, 1, far_sum, far_in.at[l]).wait_recv()
        for h in range(2):
            part = pl.ds(h * TOK, TOK)
            first = dot(pick[0, part, :], ret[l, 0])
            second = dot(pick[1, part, :], ret[l, 0])
            columns = slice(h * HALF, (h + 1) * HALF)
            stream[:, columns] = (
                stream[:, columns] + weight * first + (1.0 - weight) * second
            ) + far_in[l, part, :].astype(F32)

    def relay_combine(l):
        weight = weights[...]
        pltpu.make_async_copy(own.at[2], ret.at[l, 1], ret_r.at[l, 1]).wait()
        for h in range(2):
            part = pl.ds(h * TOK, TOK)
            first = dot(pick[0, part, :], ret[l, 1])
            second = dot(pick[1, part, :], ret[l, 1])
            far_sum[part, :] = (weight * first + (1.0 - weight) * second).astype(BF16)
        relay(l, 1, far_sum, far_in.at[l]).start()

    def prepare(l):
        codes = code_copies(l)
        for copy in codes:
            copy.wait()

        @pl.loop(0, 16)
        def _(step):
            prepare_in(l, step)

        @pl.loop(0, 8)
        def _(n):
            prepare_out(l, n)

        @pl.when(l + 1 < LAYERS)
        def _():
            for copy in code_copies(l + 1):
                copy.start()

    def gather(l, s, kind, src, dst, device):
        rows = rows_of(2 * s, 2)
        return remote(
            xf.at[(l,) + src + (rows,)], xf.at[(l,) + dst + (rows,)],
            ag_s.at[l, kind], ag_r.at[l, kind, s], device,
        )

    def up_copy(l, s):
        return gather(l, s, 1, (0, 0), (3, 0), up)

    def down_copy(l, s):
        return gather(l, s, 2, (0, 0), (1, 0), down)

    def sib_copy(l, s, d):
        return gather(l, s, {0: 0, 3: 3, 1: 4, 2: 5}[d], (d, 0), (d, 1), sibling)

    def dispatched(l, s, d):
        arrived = xf.at[l, d, 0, rows_of(2 * s, 2), :]
        pltpu.make_async_copy(arrived, arrived, disp_r.at[l, d // 2, s]).wait()

    def send_own(l, s):
        dispatched(l, s, 0)
        up_copy(l, s).start()
        down_copy(l, s).start()
        sib_copy(l, s, 0).start()

    factor = 2.0**-10 / math.sqrt(8 * WIDTH)

    def hidden_own(l, s):
        multiply_in(l, s, 0, 0, first=True)
        sib_copy(l, s, 0).wait_recv()
        multiply_in(l, s, 0, 1)

    def hidden(l, s):
        up_copy(l, s).wait_recv()
        sib_copy(l, s, 3).start()
        down_copy(l, s).wait_recv()
        sib_copy(l, s, 1).start()
        multiply_in(l, s, 3, 0)
        multiply_in(l, s, 1, 0)
        dispatched(l, s, 2)
        sib_copy(l, s, 2).start()
        multiply_in(l, s, 2, 0)
        for d in (3, 1, 2):
            sib_copy(l, s, d).wait_recv()
            multiply_in(l, s, d, 1)

        eight = scales.at[l, pl.ds(8 * s, 8)]
        pltpu.make_async_copy(eight, eight, scale_r.at[l, s]).wait()
        lanes_of = iota((CAP, TOK), 1) == iota((CAP, TOK), 0) + lax.rem(mine, 4) * 32

        zero = jnp.zeros((CAP, 128), F32)

        for j in range(8):
            first = pl.ds(j * CHUNK, CAP)
            second = pl.ds(j * CHUNK + CAP, CAP)
            scale = jnp.sum(
                jnp.where(lanes_of, scales[l, 8 * s + j, 0:1, :], 0.0), axis=1, keepdims=True
            )
            total = (acc[first, 0:256] + acc[second, 256:512]) * (factor * scale)
            gate, value = total[:, 0:128], total[:, 128:256]
            act = gate / (1.0 + jnp.exp(-gate)) * value
            actx[first, 0:128] = act
            actx[first, 128:256] = zero
            actx[second, 0:128] = zero
            actx[second, 128:256] = act

        actp[rows_of(2 * s, 2), :] = dot(actx[...].astype(BF16), mix).astype(BF16)

    def sum_sib(l, s, d):
        rows = rows_of(2 * s, 2)
        return remote(
            pk1.at[d, rows, :], sibr.at[l, d, rows, :], rs_s.at[l, 0],
            rs_r.at[l, 0, 4 * s + d], sibling,
        )

    def sum_owner(l, s, d):
        kind = 1 if d == 1 else 2
        rows = rows_of(2 * s, 2)
        return remote(
            own.at[d, rows, :], rf.at[l, kind - 1, rows, :], rs_s.at[l, kind],
            rs_r.at[l, kind, s], up if d == 1 else down,
        )

    def to_sibling(l, s, d):
        multiply_out(s, d, 1)
        sum_sib(l, s, d).start()

    def chip_sum(l, s, d):
        sum_sib(l, s, d).wait_recv()
        for g in (2 * s, 2 * s + 1):
            add_into(d, rows_of(g), [sibr.at[l, d]])

    def to_homes(l, s, d):
        which = 0 if d == 0 else 1
        for i in range(8):
            low = lax.rem(mine + i, 8)
            to_z = lax.div(low, 2)
            to_y = 2 * lax.rem(low, 2) + lax.rem(to_z + s, 2)
            src = own.at[d, chunk_at(low + 8 * s), :]
            dst = ret.at[l, which, chunk_at(mine), :]
            away = remote(
                src, dst, ret_s.at[l, which], ret_r.at[l, which],
                {"expert": to_z * 4 + to_y, "tensor": t},
            )
            if i:
                away.start()
                continue

            @pl.when(parity == s)
            def _():
                pltpu.make_async_copy(src, dst, ret_r.at[l, which]).start()

            @pl.when(parity != s)
            def _():
                away.start()

    def sums(l, s):
        to_sibling(l, s, 1)
        to_sibling(l, s, 3)
        multiply_out(s, 1, 0)
        chip_sum(l, s, 1)
        sum_owner(l, s, 1).start()
        multiply_out(s, 3, 0)
        chip_sum(l, s, 3)
        sum_owner(l, s, 3).start()
        to_sibling(l, s, 2)
        multiply_out(s, 2, 0)
        to_sibling(l, s, 0)
        chip_sum(l, s, 2)
        to_homes(l, s, 2)
        multiply_out(s, 0, 0)

    def give_back(l, s):
        sum_sib(l, s, 0).wait_recv()
        sum_owner(l, s, 1).wait_recv()
        sum_owner(l, s, 3).wait_recv()
        for g in (2 * s, 2 * s + 1):
            add_into(0, rows_of(g), [sibr.at[l, 0], rf.at[l, 0], rf.at[l, 1]])
        to_homes(l, s, 0)

    def all_sent(l):
        all_of_exchange(l).wait_send()
        fifteen = scales.at[l, pl.ds(0, 15)]
        remote(fifteen, fifteen, scale_s.at[l], scale_r.at[l, 0], sibling).wait_send()
        for kind in range(6):
            remote(
                xf.at[l, 0, 0], xf.at[l, 0, 1], ag_s.at[l, kind], ag_r.at[l, kind, 0], sibling
            ).wait_send()
        remote(pk1, sibr.at[l], rs_s.at[l, 0], rs_r.at[l, 0, 0], sibling).wait_send()
        for kind in range(1, 3):
            remote(
                own.at[1], rf.at[l, 0], rs_s.at[l, kind], rs_r.at[l, kind, 0], sibling
            ).wait_send()
        for which in range(2):
            remote(
                own.at[0, rest, :], ret.at[l, which, rest, :], ret_s.at[l, which],
                ret_r.at[l, which], sibling,
            ).wait_send()
        relay(l, 1, far_sum, far_in.at[l]).wait_send()

    def finish(l):
        combine(l)

        @pl.when(l + 1 < LAYERS)
        def _():
            dispatch_sent(l)
            send_slots(l + 1, slot_values(l + 1, True))

    def layer(l, carry):
        @pl.when((l > 0) & (parity == 0))
        def _():
            relay_slots(l)
            send_scales(l)

        @pl.when((l > 0) & (parity == 1))
        def _():
            finish(l - 1)

        send_own(l, 0)
        hidden_own(l, 0)

        @pl.when(l == 0)
        def _():
            relay_slots(0)
            send_scales(0)
            send_own(0, 1)

        @pl.when((l > 0) & (parity == 1))
        def _():
            relay_slots(l)
            send_scales(l)

        @pl.when(l > 0)
        def _():
            send_own(l, 1)

        hidden(l, 0)

        @pl.when(l > 0)
        def _():
            all_sent(l - 1)

        sums(l, 0)
        hidden_own(l, 1)
        hidden(l, 1)
        sums(l, 1)

        @pl.when(parity == 0)
        def _():
            relay_combine(l)

        give_back(l, 0)

        @pl.when(parity == 1)
        def _():
            relay_combine(l)

        give_back(l, 1)

        @pl.when(l + 1 < LAYERS)
        def _():
            prepare(l + 1)

        @pl.when(parity == 0)
        def _():
            finish(l)

        return carry

    gained = slot_values(0, False)
    pl.semaphore_wait(barrier, 22)
    relay(0, 0, xr, far_xr.at[0]).start()

    @pl.when(parity == 1)
    def _():
        prepare(0)

    send_slots(0, gained)

    @pl.when(parity == 0)
    def _():
        prepare(0)

    lane = iota((1, ROWS), 1)
    lane_chunk = lane // CHUNK
    lane_inner = lane - lane_chunk * CHUNK
    lane_half = (lane_inner >= CAP).astype(I32)
    lane_slot = lane_chunk * CAP + lane_inner - lane_half * CAP
    for k in range(2):
        for h in range(2):
            hit = (lane_half == h) & (lane_slot == slot_cols[k])
            pick[k, pl.ds(h * TOK, TOK), :] = hit.astype(F32).astype(BF16)

    lax.fori_loop(0, LAYERS, layer, 0)

    @pl.when(parity == 1)
    def _():
        combine(LAYERS - 1)

    dispatch_sent(LAYERS - 1)
    all_sent(LAYERS - 1)
    out_ref[...] = stream[...].astype(BF16)


def per_device(
    tokens, routes, norm_gain, router_weight, gate_codes, gate_scales, up_codes, up_scales,
    down_codes, down_scales,
):
    vmem = pl.BlockSpec(memory_space=pltpu.VMEM)
    anywhere = pl.BlockSpec(memory_space=pl.ANY)
    dma = pltpu.SemaphoreType.DMA
    return pl.pallas_call(
        kernel,
        out_shape=jax.ShapeDtypeStruct((TOK, WIDTH), BF16),
        in_specs=[
            vmem, vmem, vmem, vmem, anywhere, vmem, anywhere, vmem, anywhere, vmem,
        ],
        out_specs=vmem,
        scratch_shapes=[
            pltpu.VMEM((TOK, WIDTH), F32),
            pltpu.VMEM((WIDTH, WIDTH), BF16),
            pltpu.VMEM((4096, 128), I32),
            pltpu.VMEM((4096, 128), I32),
            pltpu.VMEM((64, 8192), I32),
            pltpu.VMEM((8, HALF, HALF), BF16),
            pltpu.VMEM((8, 256, HALF), BF16),
            pltpu.VMEM((ROWS, 2 * TOK), BF16),
            pltpu.VMEM((2, 2 * TOK, ROWS), BF16),
            pltpu.VMEM((2 * TOK, HALF), BF16),
            pltpu.VMEM((ROWS, HALF), BF16),
            pltpu.VMEM((LAYERS, 4, 2, ROWS, HALF), BF16),
            pltpu.VMEM((PART, HALF), F32),
            pltpu.VMEM((PART, 256), F32),
            pltpu.VMEM((ROWS, 256), BF16),
            pltpu.VMEM((4, ROWS, HALF), BF16),
            pltpu.VMEM((4, ROWS, HALF), BF16),
            pltpu.VMEM((LAYERS, 4, ROWS, HALF), BF16),
            pltpu.VMEM((LAYERS, 2, ROWS, HALF), BF16),
            pltpu.VMEM((LAYERS, 2, ROWS, HALF), BF16),
            pltpu.VMEM((LAYERS, 2 * TOK, HALF), BF16),
            pltpu.VMEM((ROWS, HALF), BF16),
            pltpu.VMEM((2 * TOK, HALF), BF16),
            pltpu.VMEM((LAYERS, 2 * TOK, HALF), BF16),
            pltpu.VMEM((LAYERS, 8, 8, TOK), F32),
            pltpu.VMEM((TOK, 1), F32),
            pltpu.VMEM((LAYERS, 4, 8, TOK), F32),
            pltpu.VMEM((LAYERS, 16, 8, TOK), F32),
            dma((3,)),
            dma((LAYERS,)), dma((LAYERS,)),
            dma((LAYERS,)), dma((LAYERS, 2)),
            dma((LAYERS, 2)), dma((LAYERS, 2, 2)),
            dma((LAYERS, 6)), dma((LAYERS, 6, 2)),
            dma((LAYERS, 3)), dma((LAYERS, 3, 8)),
            dma((LAYERS, 2)), dma((LAYERS, 2)),
            dma((LAYERS, 2)), dma((LAYERS, 2)),
        ],
        compiler_params=pltpu.CompilerParams(
            collective_id=0, has_side_effects=True, vmem_limit_bytes=60 << 20
        ),
        name="moe_layers",
    )(
        tokens, routes.T, norm_gain, router_weight.transpose(0, 2, 1),
        gate_codes.reshape(LAYERS, 4096, 128),
        gate_scales.reshape(LAYERS, 64, 128), up_codes.reshape(LAYERS, 4096, 128),
        up_scales.reshape(LAYERS, 64, 128), down_codes.reshape(LAYERS, 64, 8192),
        down_scales.reshape(LAYERS, 1, 8192),
    )


def solution(mesh):
    in_specs = (
        P("expert", "tensor"),
        P("expert", None),
        P(None, "tensor"),
        P(None, "tensor", None),
        P(None, "expert", None, "tensor"),
        P(None, "expert", None, "tensor"),
        P(None, "expert", None, "tensor"),
        P(None, "expert", None, "tensor"),
        P(None, "expert", "tensor", None),
        P(None, "expert", "tensor", None),
    )
    return jax.shard_map(
        per_device, mesh=mesh, in_specs=in_specs, out_specs=P("expert", "tensor"),
        check_vma=False,
    )
```

```python
import functools
import math

import jax
import jax.numpy as jnp
from jax import lax
from jax.experimental import pallas as pl
from jax.experimental.pallas import tpu as pltpu
from jax.sharding import PartitionSpec as P

LAYERS = 2
TOK = 128
WIDTH = 1024
HALF = 512
CAP = 24
CHUNK = 2 * CAP
ROWS = 16 * CHUNK
GROUP = 4 * CHUNK
PART = 2 * GROUP
MESH = pl.DeviceIdType.MESH
F32 = jnp.float32
BF16 = jnp.bfloat16
I32 = jnp.int32


def dot(a, b):
    return jnp.dot(a, b, preferred_element_type=F32)


def place(z, y):
    return lax.rem(z + y, 2) * 8 + z * 2 + lax.div(y, 2)


def chunk_at(index):
    return pl.ds(pl.multiple_of(index * CHUNK, CHUNK), CHUNK)


def iota(shape, dim):
    return lax.broadcasted_iota(I32, shape, dim)


def walsh(values):
    values = list(values)
    for bit in (1, 2, 4):
        for i in range(8):
            if not i & bit:
                low, high = values[i], values[i | bit]
                values[i], values[i | bit] = low + high, low - high
    return values


def rows_of(group, count=1):
    return pl.ds(group * GROUP, count * GROUP)


def kernel(
    tok_ref, routes_ref, gain_ref, rw_ref, gc_hbm, gs_ref, uc_hbm, us_ref, dc_hbm, ds_ref,
    out_ref,
    stream, had, cg, cu, cd, wp, wd, gath, pick, xr, sl, xf, acc, actx, actp,
    own, pk1, sibr, rf, ret, far_xr, far_sl, far_sum, far_in, ex, weights, scale_out, scales,
    code_sem, ex_s, ex_r, scale_s, scale_r, disp_s, disp_r, ag_s, ag_r, rs_s, rs_r, ret_s, ret_r, relay_s, relay_r,
):
    e = lax.axis_index("expert")
    t = lax.axis_index("tensor")
    z, y = lax.div(e, 4), lax.rem(e, 4)
    x, c = lax.div(t, 2), lax.rem(t, 2)
    zs = [z] + [lax.rem(z + a, 4) for a in range(1, 4)]
    ys = [y] + [lax.rem(y + b, 4) for b in range(1, 4)]
    parity = lax.rem(z + y, 2)
    mine = place(z, y)
    xs = [x * 2] + [lax.rem(x + d, 4) * 2 for d in range(1, 4)]
    cores = [c, 1 - c]

    def expert_at(a, b):
        return {"expert": zs[a] * 4 + ys[b], "tensor": t}

    def tensor_at(index):
        return {"expert": e, "tensor": index}

    def block(d, k):
        return xs[d] + cores[k]

    sibling = tensor_at(block(0, 1))
    up = tensor_at(block(1, 0))
    down = tensor_at(block(3, 0))
    across = tensor_at(block(2, 0))
    others = [tensor_at(lax.rem(t + k, 8)) for k in range(1, 8)]

    def remote(src, dst, ssem, rsem, device):
        return pltpu.make_async_remote_copy(
            src_ref=src, dst_ref=dst, send_sem=ssem, recv_sem=rsem,
            device_id=device, device_id_type=MESH,
        )

    def code_copies(l):
        return [
            pltpu.make_async_copy(gc_hbm.at[l], cg, code_sem.at[0]),
            pltpu.make_async_copy(uc_hbm.at[l], cu, code_sem.at[1]),
            pltpu.make_async_copy(dc_hbm.at[l], cd, code_sem.at[2]),
        ]

    barrier = pltpu.get_barrier_semaphore()
    for a in range(4):
        for b in range(4):
            if a or b:
                pl.semaphore_signal(
                    barrier, inc=1, device_id=expert_at(a, b), device_id_type=MESH
                )
    for other in others:
        pl.semaphore_signal(barrier, inc=1, device_id=other, device_id_type=MESH)

    for copy in code_copies(0):
        copy.start()
    eye = (iota((TOK, TOK), 0) == iota((TOK, TOK), 1)).astype(F32)
    stream[...] = tok_ref[...].astype(F32)

    def exchange_copies(l):
        return [
            remote(ex.at[l, 0], ex.at[l, k], ex_s.at[l], ex_r.at[l], others[k - 1])
            for k in range(1, 8)
        ]

    def all_of_exchange(l):
        seven = ex.at[l, pl.ds(1, 7)]
        return remote(seven, seven, ex_s.at[l], ex_r.at[l], sibling)

    def as_row(column):
        return jnp.sum(eye * column, axis=0, keepdims=True)

    def as_column(row):
        return jnp.sum(eye * row, axis=1, keepdims=True)

    below = (iota((TOK, TOK), 0) > iota((TOK, TOK), 1)).astype(BF16)
    lanes = iota((TOK, 16), 1)
    picks, rels = [], []
    for k in range(2):
        named = jnp.sum(
            eye * routes_ref[k : k + 1, :].astype(F32), axis=1, keepdims=True
        ).astype(I32)
        picks.append((named == lanes).astype(F32))
        to_z, to_y = named >> 2, named & 3
        rels.append(((to_z + to_y) & 1) * 8 + to_z * 2 + (to_y >> 1))
    earlier = dot(below, (picks[0] + picks[1]).astype(BF16))
    slots = []
    for k in range(2):
        rank = jnp.sum(picks[k] * earlier, axis=1, keepdims=True)
        slots.append(rels[k].astype(F32) * CAP + rank)
    slot_rows = [as_row(s).astype(I32) for s in slots]
    slot_cols = [s.astype(I32) for s in slots]
    sign = picks[0] - picks[1]

    row = iota((ROWS, 1), 0)
    chunk = row // CHUNK
    inner = row - chunk * CHUNK
    row_half = (inner >= CAP).astype(I32)
    row_slot = chunk * CAP + inner - row_half * CAP
    col_half = (iota((1, 2 * TOK), 1) >= TOK).astype(I32)
    both = [jnp.concatenate([s, s], axis=1) for s in slot_rows]
    hit = (row_half == col_half) & ((row_slot == both[0]) | (row_slot == both[1]))
    gath[...] = hit.astype(F32).astype(BF16)

    @pl.loop(0, 32)
    def _(i):
        at = pl.multiple_of(i * 32, 32)
        r = iota((32, WIDTH), 0) + at
        j = iota((32, WIDTH), 1)
        v = r & (2 * (j & (HALF - 1)) + (j >> 9))
        v = v ^ (v >> 8)
        v = v ^ (v >> 4)
        v = v ^ (v >> 2)
        v = v ^ (v >> 1)
        had[pl.ds(at, 32), :] = (1 - 2 * (v & 1)).astype(F32).astype(BF16)

    def prepare_in(l, step):
        at = pl.multiple_of(step * 32, 32)
        for kind, (codes, scales) in enumerate(((cg, gs_ref), (cu, us_ref))):
            words = [codes[pl.ds(m * HALF + at, 32), :] for m in range(8)]
            shifts = [10 - scales[l, pl.ds(m * 8 + step // 2, 1), :] for m in range(8)]
            for k in range(2):
                values = walsh(
                    ((((w >> (4 * k)) & 15) - 8) << s) for w, s in zip(words, shifts)
                )
                column = k * 256 + kind * 128
                for n in range(8):
                    wp[n, pl.ds(at, 32), column : column + 128] = (
                        values[n].astype(F32).astype(BF16)
                    )

    def prepare_out(l, n):
        for h in range(2):
            at = pl.multiple_of(n * WIDTH + h * HALF, HALF)
            words = cd[:, pl.ds(at, HALF)]
            shift = 8 - ds_ref[l, :, pl.ds(at, HALF)]
            for k in range(2):
                value = (((words >> (4 * k)) & 15) - 8) << shift
                wd[n, pl.ds(h * 128 + k * 64, 64), :] = (
                    value.astype(F32) * (2.0**-8)
                ).astype(BF16)

    def multiply_in(l, s, d, k, first=False):
        value = dot(xf[l, d, k, rows_of(2 * s, 2), :], wp[block(d, k)])
        if first:
            acc[...] = value
        else:
            acc[...] += value

    def multiply_out(s, d, k):
        target = own if k == 0 else pk1
        rows = rows_of(2 * s, 2)
        target[d, rows, :] = dot(actp[rows, :], wd[block(d, k)]).astype(BF16)

    def add_into(d, rows, parts):
        total = own[d, rows, :].astype(F32)
        for part in parts:
            total = total + part[rows, :].astype(F32)
        own[d, rows, :] = total.astype(BF16)

    mix = (
        (iota((256, 256), 0) >> 7 == iota((256, 256), 1) >> 7)
        & (
            iota((256, 256), 1) & 127
            == ((iota((256, 256), 0) & 127) >> 1) + 64 * (iota((256, 256), 0) & 1)
        )
    ).astype(F32).astype(BF16)

    hops = sorted(
        ((a, b) for a in range(4) for b in range(4) if a or b),
        key=lambda ab: -(min(ab[0], 4 - ab[0]) + min(ab[1], 4 - ab[1])),
    )
    targets = [(expert_at(a, b), place(zs[a], ys[b])) for a, b in hops]
    rest = pl.ds(CHUNK, ROWS - CHUNK)

    def relay(l, step, src, dst):
        return remote(src, dst, relay_s.at[l, step], relay_r.at[l, step], across)

    def dispatch_sent(l):
        relay(l, 0, xr, far_xr.at[l]).wait_send()
        remote(
            far_sl.at[rest, :], xf.at[l, 2, 0, rest, :], disp_s.at[l, 1], disp_r.at[l, 1, 0],
            sibling,
        ).wait_send()
        remote(
            sl.at[rest, :], xf.at[l, 0, 0, rest, :], disp_s.at[l, 0], disp_r.at[l, 0, 0],
            sibling,
        ).wait_send()

    def slot_values(l, ready):
        gained = (stream[...] * gain_ref[pl.ds(l, 1), :]).astype(BF16)
        turned = dot(gained, had[...]).astype(BF16)
        for h in range(2):
            xr[pl.ds(h * TOK, TOK), :] = turned[:, h * HALF : (h + 1) * HALF]

        if ready:
            relay(l, 0, xr, far_xr.at[l]).start()
        sl[...] = dot(gath[...], xr[...]).astype(BF16)
        return gained

    def to_experts(l, d, rows):
        which = 0 if d == 0 else 1
        for device, index in targets:
            remote(
                rows.at[chunk_at(index), :], xf.at[l, d, 0, chunk_at(mine), :],
                disp_s.at[l, which], disp_r.at[l, which, parity], device,
            ).start()
        pltpu.make_async_copy(
            rows.at[chunk_at(mine), :], xf.at[l, d, 0, chunk_at(mine), :],
            disp_r.at[l, which, parity],
        ).start()

    def relay_slots(l):
        relay(l, 0, xr, far_xr.at[l]).wait_recv()
        far_sl[...] = dot(gath[...], far_xr[l]).astype(BF16)
        to_experts(l, 2, far_sl)

    def send_slots(l, gained):
        to_experts(l, 0, sl)
        st = stream[...]
        squares = jnp.sum(st * st, axis=1, keepdims=True)
        logits = lax.dot_general(
            gained, rw_ref[l], (((1,), (1,)), ((), ())), preferred_element_type=F32
        )
        diff = jnp.sum(logits * sign, axis=1, keepdims=True)
        ex[l, 0] = jnp.where(iota((8, TOK), 0) == 0, as_row(squares), as_row(diff))
        for copy in exchange_copies(l):
            copy.start()

    def send_scales(l):
        all_of_exchange(l).wait_recv()
        total = ex[l, 0]
        for k in range(1, 8):
            total = total + ex[l, k]
        factor = lax.rsqrt(as_column(total[0:1, :]) / (8 * WIDTH) + 1e-05)
        weights[...] = 1.0 / (1.0 + jnp.exp(-factor * as_column(total[1:2, :])))
        at = iota((TOK, TOK), 1)
        for p in range(4):
            slot = (p * 4 + (at >> 5)) * CAP + (at & 31)
            hit = ((slot == slot_cols[0]) | (slot == slot_cols[1])) & ((at & 31) < CAP)
            row = jnp.sum(jnp.where(hit, factor, 0.0), axis=0, keepdims=True)
            scale_out[l, p] = jnp.broadcast_to(row, (8, TOK))
        for device, index in targets:
            remote(
                scale_out.at[l, lax.div(index, 4)], scales.at[l, mine], scale_s.at[l],
                scale_r.at[l, parity], device,
            ).start()
        pltpu.make_async_copy(
            scale_out.at[l, lax.div(mine, 4)], scales.at[l, mine], scale_r.at[l, parity]
        ).start()

    def combine(l):
        weight = weights[...]
        pltpu.make_async_copy(own.at[0], ret.at[l, 0], ret_r.at[l, 0]).wait()
        picked = dot(pick[...], ret[l, 0])
        relay(l, 1, far_sum, far_in.at[l]).wait_recv()
        for h in range(2):
            part = pl.ds(h * TOK, TOK)
            first = picked[h * TOK : (h + 1) * TOK]
            second = picked[(2 + h) * TOK : (3 + h) * TOK]
            columns = slice(h * HALF, (h + 1) * HALF)
            stream[:, columns] = (
                stream[:, columns] + weight * first + (1.0 - weight) * second
            ) + far_in[l, part, :].astype(F32)

    def relay_combine(l):
        weight = weights[...]
        pltpu.make_async_copy(own.at[2], ret.at[l, 1], ret_r.at[l, 1]).wait()
        picked = dot(pick[...], ret[l, 1])
        for h in range(2):
            part = pl.ds(h * TOK, TOK)
            first = picked[h * TOK : (h + 1) * TOK]
            second = picked[(2 + h) * TOK : (3 + h) * TOK]
            far_sum[part, :] = (weight * first + (1.0 - weight) * second).astype(BF16)
        relay(l, 1, far_sum, far_in.at[l]).start()

    def prepare(l):
        codes = code_copies(l)
        for copy in codes:
            copy.wait()

        @pl.loop(0, 16)
        def _(step):
            prepare_in(l, step)

        @pl.loop(0, 8)
        def _(n):
            prepare_out(l, n)

        @pl.when(l + 1 < LAYERS)
        def _():
            for copy in code_copies(l + 1):
                copy.start()

    def gather(l, s, kind, src, dst, device):
        rows = rows_of(2 * s, 2)
        return remote(
            xf.at[(l,) + src + (rows,)], xf.at[(l,) + dst + (rows,)],
            ag_s.at[l, kind], ag_r.at[l, kind, s], device,
        )

    def up_copy(l, s):
        return gather(l, s, 1, (0, 0), (3, 0), up)

    def down_copy(l, s):
        return gather(l, s, 2, (0, 0), (1, 0), down)

    def sib_copy(l, s, d):
        return gather(l, s, {0: 0, 3: 3, 1: 4, 2: 5}[d], (d, 0), (d, 1), sibling)

    def dispatched(l, s, d):
        arrived = xf.at[l, d, 0, rows_of(2 * s, 2), :]
        pltpu.make_async_copy(arrived, arrived, disp_r.at[l, d // 2, s]).wait()

    def send_own(l, s):
        dispatched(l, s, 0)
        up_copy(l, s).start()
        down_copy(l, s).start()
        sib_copy(l, s, 0).start()

    factor = 2.0**-10 / math.sqrt(8 * WIDTH)

    def hidden_own(l, s):
        multiply_in(l, s, 0, 0, first=True)
        sib_copy(l, s, 0).wait_recv()
        multiply_in(l, s, 0, 1)

    def hidden(l, s):
        up_copy(l, s).wait_recv()
        sib_copy(l, s, 3).start()
        down_copy(l, s).wait_recv()
        sib_copy(l, s, 1).start()
        multiply_in(l, s, 3, 0)
        multiply_in(l, s, 1, 0)
        dispatched(l, s, 2)
        sib_copy(l, s, 2).start()
        multiply_in(l, s, 2, 0)
        for d in (3, 1, 2):
            sib_copy(l, s, d).wait_recv()
            multiply_in(l, s, d, 1)

        eight = scales.at[l, pl.ds(8 * s, 8)]
        pltpu.make_async_copy(eight, eight, scale_r.at[l, s]).wait()
        lanes_of = iota((CAP, TOK), 1) == iota((CAP, TOK), 0) + lax.rem(mine, 4) * 32

        zero = jnp.zeros((CAP, 128), F32)

        for j in range(8):
            first = pl.ds(j * CHUNK, CAP)
            second = pl.ds(j * CHUNK + CAP, CAP)
            scale = jnp.sum(
                jnp.where(lanes_of, scales[l, 8 * s + j, 0:1, :], 0.0), axis=1, keepdims=True
            )
            total = (acc[first, 0:256] + acc[second, 256:512]) * (factor * scale)
            gate, value = total[:, 0:128], total[:, 128:256]
            act = gate / (1.0 + jnp.exp(-gate)) * value
            actx[first, 0:128] = act
            actx[first, 128:256] = zero
            actx[second, 0:128] = zero
            actx[second, 128:256] = act

        actp[rows_of(2 * s, 2), :] = dot(actx[...].astype(BF16), mix).astype(BF16)

    def sum_sib(l, s, d):
        rows = rows_of(2 * s, 2)
        return remote(
            pk1.at[d, rows, :], sibr.at[l, d, rows, :], rs_s.at[l, 0],
            rs_r.at[l, 0, 4 * s + d], sibling,
        )

    def sum_owner(l, s, d):
        kind = 1 if d == 1 else 2
        rows = rows_of(2 * s, 2)
        return remote(
            own.at[d, rows, :], rf.at[l, kind - 1, rows, :], rs_s.at[l, kind],
            rs_r.at[l, kind, s], up if d == 1 else down,
        )

    def to_sibling(l, s, d):
        multiply_out(s, d, 1)
        sum_sib(l, s, d).start()

    def chip_sum(l, s, d):
        sum_sib(l, s, d).wait_recv()
        for g in (2 * s, 2 * s + 1):
            add_into(d, rows_of(g), [sibr.at[l, d]])

    def to_homes(l, s, d):
        which = 0 if d == 0 else 1
        for i in range(8):
            low = lax.rem(mine + i, 8)
            to_z = lax.div(low, 2)
            to_y = 2 * lax.rem(low, 2) + lax.rem(to_z + s, 2)
            src = own.at[d, chunk_at(low + 8 * s), :]
            dst = ret.at[l, which, chunk_at(mine), :]
            away = remote(
                src, dst, ret_s.at[l, which], ret_r.at[l, which],
                {"expert": to_z * 4 + to_y, "tensor": t},
            )
            if i:
                away.start()
                continue

            @pl.when(parity == s)
            def _():
                pltpu.make_async_copy(src, dst, ret_r.at[l, which]).start()

            @pl.when(parity != s)
            def _():
                away.start()

    def sums(l, s):
        to_sibling(l, s, 1)
        to_sibling(l, s, 3)
        multiply_out(s, 1, 0)
        chip_sum(l, s, 1)
        sum_owner(l, s, 1).start()
        multiply_out(s, 3, 0)
        chip_sum(l, s, 3)
        sum_owner(l, s, 3).start()
        to_sibling(l, s, 2)
        multiply_out(s, 2, 0)
        to_sibling(l, s, 0)
        chip_sum(l, s, 2)
        to_homes(l, s, 2)
        multiply_out(s, 0, 0)

    def give_back(l, s):
        sum_sib(l, s, 0).wait_recv()
        sum_owner(l, s, 1).wait_recv()
        sum_owner(l, s, 3).wait_recv()
        for g in (2 * s, 2 * s + 1):
            add_into(0, rows_of(g), [sibr.at[l, 0], rf.at[l, 0], rf.at[l, 1]])
        to_homes(l, s, 0)

    def all_sent(l):
        all_of_exchange(l).wait_send()
        fifteen = scales.at[l, pl.ds(0, 15)]
        remote(fifteen, fifteen, scale_s.at[l], scale_r.at[l, 0], sibling).wait_send()
        for kind in range(6):
            remote(
                xf.at[l, 0, 0], xf.at[l, 0, 1], ag_s.at[l, kind], ag_r.at[l, kind, 0], sibling
            ).wait_send()
        remote(pk1, sibr.at[l], rs_s.at[l, 0], rs_r.at[l, 0, 0], sibling).wait_send()
        for kind in range(1, 3):
            remote(
                own.at[1], rf.at[l, 0], rs_s.at[l, kind], rs_r.at[l, kind, 0], sibling
            ).wait_send()
        for which in range(2):
            remote(
                own.at[0, rest, :], ret.at[l, which, rest, :], ret_s.at[l, which],
                ret_r.at[l, which], sibling,
            ).wait_send()
        relay(l, 1, far_sum, far_in.at[l]).wait_send()

    def finish(l):
        combine(l)

        @pl.when(l + 1 < LAYERS)
        def _():
            dispatch_sent(l)
            send_slots(l + 1, slot_values(l + 1, True))

    def layer(l, carry):
        @pl.when((l > 0) & (parity == 0))
        def _():
            relay_slots(l)
            send_scales(l)

        @pl.when((l > 0) & (parity == 1))
        def _():
            finish(l - 1)

        send_own(l, 0)
        hidden_own(l, 0)

        @pl.when(l == 0)
        def _():
            relay_slots(0)
            send_scales(0)
            send_own(0, 1)

        @pl.when((l > 0) & (parity == 1))
        def _():
            relay_slots(l)
            send_scales(l)

        @pl.when(l > 0)
        def _():
            send_own(l, 1)

        hidden(l, 0)

        @pl.when(l > 0)
        def _():
            all_sent(l - 1)

        sums(l, 0)
        hidden_own(l, 1)
        hidden(l, 1)
        sums(l, 1)

        @pl.when(parity == 0)
        def _():
            relay_combine(l)

        give_back(l, 0)

        @pl.when(parity == 1)
        def _():
            relay_combine(l)

        give_back(l, 1)

        @pl.when(l + 1 < LAYERS)
        def _():
            prepare(l + 1)

        @pl.when(parity == 0)
        def _():
            finish(l)

        return carry

    gained = slot_values(0, False)
    pl.semaphore_wait(barrier, 22)
    relay(0, 0, xr, far_xr.at[0]).start()

    @pl.when(parity == 1)
    def _():
        prepare(0)

    send_slots(0, gained)

    @pl.when(parity == 0)
    def _():
        prepare(0)

    lane = iota((1, ROWS), 1)
    lane_chunk = lane // CHUNK
    lane_inner = lane - lane_chunk * CHUNK
    lane_half = (lane_inner >= CAP).astype(I32)
    lane_slot = lane_chunk * CAP + lane_inner - lane_half * CAP
    for k in range(2):
        for h in range(2):
            hit = (lane_half == h) & (lane_slot == slot_cols[k])
            pick[pl.ds((2 * k + h) * TOK, TOK), :] = hit.astype(F32).astype(BF16)

    lax.fori_loop(0, LAYERS, layer, 0)

    @pl.when(parity == 1)
    def _():
        combine(LAYERS - 1)

    dispatch_sent(LAYERS - 1)
    all_sent(LAYERS - 1)
    out_ref[...] = stream[...].astype(BF16)


def per_device(
    tokens, routes, norm_gain, router_weight, gate_codes, gate_scales, up_codes, up_scales,
    down_codes, down_scales,
):
    vmem = pl.BlockSpec(memory_space=pltpu.VMEM)
    anywhere = pl.BlockSpec(memory_space=pl.ANY)
    dma = pltpu.SemaphoreType.DMA
    return pl.pallas_call(
        kernel,
        out_shape=jax.ShapeDtypeStruct((TOK, WIDTH), BF16),
        in_specs=[
            vmem, vmem, vmem, vmem, anywhere, vmem, anywhere, vmem, anywhere, vmem,
        ],
        out_specs=vmem,
        scratch_shapes=[
            pltpu.VMEM((TOK, WIDTH), F32),
            pltpu.VMEM((WIDTH, WIDTH), BF16),
            pltpu.VMEM((4096, 128), I32),
            pltpu.VMEM((4096, 128), I32),
            pltpu.VMEM((64, 8192), I32),
            pltpu.VMEM((8, HALF, HALF), BF16),
            pltpu.VMEM((8, 256, HALF), BF16),
            pltpu.VMEM((ROWS, 2 * TOK), BF16),
            pltpu.VMEM((4 * TOK, ROWS), BF16),
            pltpu.VMEM((2 * TOK, HALF), BF16),
            pltpu.VMEM((ROWS, HALF), BF16),
            pltpu.VMEM((LAYERS, 4, 2, ROWS, HALF), BF16),
            pltpu.VMEM((PART, HALF), F32),
            pltpu.VMEM((PART, 256), F32),
            pltpu.VMEM((ROWS, 256), BF16),
            pltpu.VMEM((4, ROWS, HALF), BF16),
            pltpu.VMEM((4, ROWS, HALF), BF16),
            pltpu.VMEM((LAYERS, 4, ROWS, HALF), BF16),
            pltpu.VMEM((LAYERS, 2, ROWS, HALF), BF16),
            pltpu.VMEM((LAYERS, 2, ROWS, HALF), BF16),
            pltpu.VMEM((LAYERS, 2 * TOK, HALF), BF16),
            pltpu.VMEM((ROWS, HALF), BF16),
            pltpu.VMEM((2 * TOK, HALF), BF16),
            pltpu.VMEM((LAYERS, 2 * TOK, HALF), BF16),
            pltpu.VMEM((LAYERS, 8, 8, TOK), F32),
            pltpu.VMEM((TOK, 1), F32),
            pltpu.VMEM((LAYERS, 4, 8, TOK), F32),
            pltpu.VMEM((LAYERS, 16, 8, TOK), F32),
            dma((3,)),
            dma((LAYERS,)), dma((LAYERS,)),
            dma((LAYERS,)), dma((LAYERS, 2)),
            dma((LAYERS, 2)), dma((LAYERS, 2, 2)),
            dma((LAYERS, 6)), dma((LAYERS, 6, 2)),
            dma((LAYERS, 3)), dma((LAYERS, 3, 8)),
            dma((LAYERS, 2)), dma((LAYERS, 2)),
            dma((LAYERS, 2)), dma((LAYERS, 2)),
        ],
        compiler_params=pltpu.CompilerParams(
            collective_id=0, has_side_effects=True, vmem_limit_bytes=60 << 20
        ),
        name="moe_layers",
    )(
        tokens, routes.T, norm_gain, router_weight.transpose(0, 2, 1),
        gate_codes.reshape(LAYERS, 4096, 128),
        gate_scales.reshape(LAYERS, 64, 128), up_codes.reshape(LAYERS, 4096, 128),
        up_scales.reshape(LAYERS, 64, 128), down_codes.reshape(LAYERS, 64, 8192),
        down_scales.reshape(LAYERS, 1, 8192),
    )


def solution(mesh):
    in_specs = (
        P("expert", "tensor"),
        P("expert", None),
        P(None, "tensor"),
        P(None, "tensor", None),
        P(None, "expert", None, "tensor"),
        P(None, "expert", None, "tensor"),
        P(None, "expert", None, "tensor"),
        P(None, "expert", None, "tensor"),
        P(None, "expert", "tensor", None),
        P(None, "expert", "tensor", None),
    )
    return jax.shard_map(
        per_device, mesh=mesh, in_specs=in_specs, out_specs=P("expert", "tensor"),
        check_vma=False,
    )
```
